32 devices in a mesh: gx: 4 (over z), gy: 8 (over y, x, core).
Axes of the slice: x: 2, y: 2, z: 4, core: 2. Of those that a mesh axis runs over, the one named last changes fastest.
Arguments:
- outer_state: bfloat16 [5, 64, 16, 8192], P(None, None, 'gy', 'gx'), may hold values from -6 to 6
- derivative: bfloat16 [3, 64, 64], replicated, may hold values from -0.75 to 0.75
- stiffness: float32 [64, 64], replicated, may hold values from -0.75 to 0.75
- wall_rhs: float32 [1024, 320], P(('gx', 'gy')), may hold values from -6 to 6
- wall_sigma: float32 [1024, 320], P(('gx', 'gy')), may hold values from 0.2 to 5
- wall_inverse: bfloat16 [1024, 320, 320], P(('gx', 'gy')), as said below
- wall_count: int32 [4, 8], P('gx', 'gy'), may hold values from 1 to 32, as said below
Outputs:
- outer_residual: bfloat16 [5, 64, 16, 8192], P(None, None, 'gy', 'gx')
- wall_update: float32 [1024, 320], P(('gx', 'gy'))
The draws below stay inside these ranges and needn't reach their ends.
Inputs may be any that keep to these rules, and one draw needn't show every extreme that they name: `wall_count`: live near-wall elements fill the first slots of a device; every device with gy index 0 holds 32, every other at most 8. `wall_inverse`: every block is invertible.
All inputs are finite; a program needn't handle non-finite values.
Results may differ from the reference program's by a relative error of at most 0.0045.
Values may be sent and summed in bfloat16 or wider, within the bound.
No kernel may reach another device: no remote copies, remote signals or barrier semaphores. Data moves between devices by JAX's collectives and lax.ppermute only.
A program may use at most 128 MiB of HBM per device.

```python
import math
import jax
import jax.numpy as jnp
from jax import lax

Q = 4
NV = 5
NP = 64
BS = 320
EX_DEV = 2048
EY_DEV = 2
WB_DEV = 32
ITERS = 3
SPAN_X = 4
SPAN_Y = 8
ROWS = 16
COLUMNS = 8192
WALLS = 1024
N_GX = 4
N_GY = 8


def draw_wall_inverse(key, part):
    first_key, second_key = jax.random.split(jax.random.fold_in(key, 11))
    diagonal = jnp.exp(jax.random.uniform(first_key, (WALLS, BS, 1), jnp.float32, jnp.log(0.5), jnp.log(2.0)))
    noise = jax.random.normal(second_key, (WALLS, BS, BS), jnp.float32) * (0.5 / jnp.sqrt(float(BS)))
    identity = (jnp.arange(BS)[:, None] == jnp.arange(BS)[None, :]).astype(jnp.float32)
    return (noise + diagonal * identity[None]).astype(jnp.bfloat16)


def draw_wall_count(key, part):
    others = jax.random.randint(jax.random.fold_in(key, 23), (SPAN_X, SPAN_Y), 1, WB_DEV // 4 + 1)
    column = jnp.arange(SPAN_Y)[None, :]
    return jnp.where(column == 0, WB_DEV, others).astype(jnp.int32)


def block_levels(rng, shape, cuts, smallest, high):
    gain, own = 1.0, jax.random.fold_in(rng, 6)
    for axis_at, shards_of in cuts:
        heights = jnp.exp(jax.random.uniform(jax.random.fold_in(own, axis_at), (shards_of,), jnp.float32, smallest / len(cuts), high / len(cuts)))
        gain = gain * jnp.repeat(heights, shape[axis_at] // shards_of).reshape([-1 if axis == axis_at else 1 for axis in range(len(shape))])
    return gain


def scatter_about(stream_key, dims, spread, bound, shards=(), held_as=jnp.bfloat16):
    values = jax.random.normal(stream_key, dims, jnp.float32) * spread
    if len(shards) > 0:
        values = block_levels(stream_key, dims, shards, -0.22, 0.18) * values
    return jnp.clip(values, min=-bound, max=bound).astype(held_as)


def setup_inputs(seed: int = 0) -> dict:
    seeds = jax.random.split(jax.random.key(seed), 8)
    return {
        "outer_state": scatter_about(seeds[0], (NV, NP, ROWS, COLUMNS), 1.0, 6.0, ((2, 8), (3, 4))),
        "derivative": scatter_about(seeds[1], (3, NP, NP), NP ** -0.5, 0.75),
        "stiffness": scatter_about(seeds[2], (NP, NP), NP ** -0.5, 0.75, (), jnp.float32),
        "wall_rhs": scatter_about(seeds[3], (WALLS, BS), 1.0, 6.0, ((0, 32),), jnp.float32),
        "wall_sigma": jnp.clip(jnp.exp(math.log(5.0) - 3.218876 * jax.random.uniform(seeds[4], (WALLS, BS), jnp.float32) ** block_levels(seeds[4], (WALLS, BS), ((0, 32),), -0.2, 0.2)), 0.2, 5.0),
        "wall_inverse": draw_wall_inverse(jax.random.fold_in(seeds[7], 71), 0),
        "wall_count": draw_wall_count(jax.random.fold_in(seeds[7], 71), 0),
    }


time_step = 0.3
coupling = 0.25
upwind_x = 2.0
upwind_y = 1.0
advection = (1.0, 0.5, 0.25)

def volume_of(part_state, derivative):
    state = part_state.astype(jnp.float32)
    fluxes = jnp.stack([state * (advection[d] + state[1 + d]) for d in range(3)]).astype(jnp.bfloat16)
    return jnp.einsum('dmn,dvnyx->vmyx', derivative.astype(jnp.float32), fluxes.astype(jnp.float32))

def least_squares(hess, beta):
    gram = jnp.dot(hess.T, hess, precision=lax.Precision.HIGHEST)
    target = beta * hess[0]
    lower = jnp.linalg.cholesky(gram)
    middle = lax.linalg.triangular_solve(lower, target[:, None], left_side=True, lower=True)
    return lax.linalg.triangular_solve(lower, middle, left_side=True, lower=True, transpose_a=True)[:, 0]

def reference(outer_state, derivative, stiffness, wall_rhs, wall_sigma, wall_inverse, wall_count):
    blocks = outer_state.reshape(NV, NP, ROWS, N_GX, EX_DEV).transpose(3, 0, 1, 2, 4)
    parts = lax.map(lambda piece: volume_of(piece, derivative), blocks)
    volume = parts.transpose(1, 2, 3, 0, 4).reshape(NV, NP, ROWS, COLUMNS)
    cube = outer_state.reshape(NV, Q, Q, Q, ROWS, COLUMNS).astype(jnp.float32)
    upstream_x = jnp.roll(cube[:, :, :, Q - 1], 1, axis=-1)
    jump_x = upstream_x - cube[:, :, :, 0]
    top = cube[:, :, Q - 1]
    upstream_y = jnp.concatenate([jnp.zeros_like(top[:, :, :, :1]), top[:, :, :, :-1]], axis=3)
    jump_y = upstream_y - cube[:, :, 0]
    resid = volume.reshape(NV, Q, Q, Q, ROWS, COLUMNS)
    resid = resid.at[:, :, :, 0].add(upwind_x * jump_x)
    resid = resid.at[:, :, 0].add(upwind_y * jump_y)
    resid = resid.reshape(NV, NP, ROWS, COLUMNS)
    outer_residual = resid.astype(jnp.bfloat16)
    trace = resid[:, :, ::EY_DEV, :].reshape(NV, NP, N_GY, N_GX, EX_DEV)[..., :WB_DEV]
    trace = trace.transpose(3, 2, 4, 0, 1).reshape(WALLS, BS)
    slots = jnp.arange(WB_DEV, dtype=jnp.int32)
    live = (slots[None, None, :] < wall_count[:, :, None]).astype(jnp.float32).reshape(WALLS)

    def operate(vectors):
        stiff = jnp.einsum('wvn,nm->wvm', vectors.reshape(WALLS, NV, NP), stiffness, precision=lax.Precision.HIGHEST).reshape(WALLS, BS)
        grid = vectors.reshape(N_GX, N_GY * WB_DEV, BS)
        beside = (jnp.roll(grid, 1, axis=0) + jnp.roll(grid, -1, axis=0)).reshape(WALLS, BS)
        return live[:, None] * (vectors + time_step * (wall_sigma * vectors + stiff) - coupling * beside)

    def precondition(vectors):
        pieces = (wall_inverse.reshape(N_GX * N_GY, WB_DEV, BS, BS), vectors.reshape(N_GX * N_GY, WB_DEV, BS))
        applied = lax.map(lambda pair: jnp.einsum('wij,wj->wi', pair[0].astype(jnp.float32), pair[1], precision=lax.Precision.HIGHEST), pieces)
        return applied.reshape(WALLS, BS)
    rhs = live[:, None] * (wall_rhs + time_step * trace)
    beta = jnp.sqrt(jnp.sum(rhs * rhs))
    basis = [rhs / beta]
    directions = []
    columns = []
    for column_index in range(ITERS):
        direction = precondition(basis[column_index])
        directions.append(direction)
        image = operate(direction)
        entries = []
        for row_index in range(column_index + 1):
            value = jnp.sum(image * basis[row_index])
            image = image - value * basis[row_index]
            entries.append(value)
        length = jnp.sqrt(jnp.sum(image * image))
        entries.append(length)
        basis.append(image / length)
        columns.append(jnp.concatenate([jnp.stack(entries), jnp.zeros((ITERS - column_index - 1,), jnp.float32)]))
    hess = jnp.stack(columns, axis=1)
    weights = least_squares(hess, beta)
    wall_update = jnp.zeros((WALLS, BS), jnp.float32)
    for column_index in range(ITERS):
        wall_update = wall_update + weights[column_index] * directions[column_index]
    return (outer_residual, wall_update)
```

```python
import jax
import jax.numpy as jnp
import numpy as np
from jax import lax
from jax.experimental import pallas as pl
from jax.experimental.pallas import tpu as pltpu
from jax.sharding import PartitionSpec as P

Q = 4
ITERS = 3

time_step = 0.3
coupling = 0.25
upwind_x = 2.0
upwind_y = 1.0
advection = (1.0, 0.5, 0.25)

LANES = 128
GROUP = 8
VMEM_BYTES = 24 << 20
bf16 = jnp.bfloat16
f32 = jnp.float32

in_vmem = pl.BlockSpec(memory_space=pltpu.VMEM)
in_hbm = pl.BlockSpec(memory_space=pltpu.HBM)
in_smem = pl.BlockSpec(memory_space=pltpu.SMEM)
params = pltpu.CompilerParams(vmem_limit_bytes=VMEM_BYTES)


def held_in_hbm(array):
    return pltpu.with_memory_space_constraint(array, pltpu.HBM)


def ring(axis, by):
    count = lax.axis_size(axis)
    return [(i, (i + by) % count) for i in range(count)]


def from_below(array, axis):
    count = lax.axis_size(axis)
    return lax.ppermute(array, axis, [(i, i + 1) for i in range(count - 1)])


def neighbours(array, axis):
    count = lax.axis_size(axis)
    if count % 2 or count < 4:
        return lax.ppermute(array, axis, ring(axis, 1)), lax.ppermute(array, axis, ring(axis, -1))
    even = [(i, i ^ 1) for i in range(count)]
    odd = [(i, (i + (1 if i % 2 else -1)) % count) for i in range(count)]
    return lax.ppermute(array, axis, even), lax.ppermute(array, axis, odd)


def jump_matrix(nodes, rows):
    faces = nodes // Q
    out = np.zeros((nodes * rows, nodes * rows + 2 * faces * rows), np.float32)
    for m in range(nodes):
        i, j, k = m % Q, m // Q % Q, m // (Q * Q)
        for r in range(rows):
            row = m * rows + r
            if i == 0:
                out[row, row] -= upwind_x
                out[row, nodes * rows + (m // Q) * rows + r] += upwind_x
            if j == 0:
                out[row, row] -= upwind_y
                if r > 0:
                    out[row, (m + Q * (Q - 1)) * rows + r - 1] += upwind_y
                else:
                    column = (k * Q + i) * rows + rows - 1
                    out[row, (nodes + faces) * rows + column] += upwind_y
    return out


def tile_view(array):
    *lead, rows, cols = array.shape
    return jnp.swapaxes(array.reshape(*lead, rows, cols // LANES, LANES), -3, -2)


def from_tile_view(array):
    *lead, tiles, rows, lanes = array.shape
    return jnp.swapaxes(array, -3, -2).reshape(*lead, rows, tiles * lanes)


def faces_kernel(state_ref, edge_ref, corner_ref, top_ref, sem):
    comps, _, _, tiles, rows, lanes = state_ref.shape
    top = [
        pltpu.make_async_copy(
            state_ref.at[:, pl.ds(k * Q + Q - 1, 1), :, t], top_ref.at[t, :, pl.ds(k, 1)], sem.at[2 + Q + t * Q + k]
        )
        for t in range(tiles)
        for k in range(Q)
    ]
    copies = [pltpu.make_async_copy(state_ref.at[:, :, Q - 1, tiles - 1], edge_ref, sem.at[0])]
    copies += [
        pltpu.make_async_copy(
            state_ref.at[:, pl.ds(k * Q + Q - 1, 1), :, 0], corner_ref.at[:, pl.ds(k, 1)], sem.at[1 + k]
        )
        for k in range(Q)
    ]
    for copy in copies + top:
        copy.start()
    for copy in copies + top:
        copy.wait()


def prep_kernel(
    state_ref, blocks_ref, rhs_ref, sigma_ref, deriv_ref, stiff_ref, expand_ref, jump_ref,
    tiles_ref, blocks_out_ref, rhs_out_ref, sigma_out_ref, full_ref, first_ref, block_ref,
    deriv_in, stiff_in, expand_in, jump_in, sem,
):
    count = tiles_ref.shape[0]
    small = [
        pltpu.make_async_copy(source, target, sem.at[at])
        for at, (source, target) in enumerate([
            (deriv_ref, deriv_in), (expand_ref, expand_in), (jump_ref, jump_in), (stiff_ref, stiff_in),
            (rhs_ref, rhs_out_ref), (sigma_ref, sigma_out_ref), (blocks_ref, blocks_out_ref),
        ])
    ]
    large = [
        pltpu.make_async_copy(state_ref.at[:, :, :, t], tiles_ref.at[t], sem.at[len(small) + t]) for t in range(count)
    ]
    for copy in small[:-1] + large + small[-1:]:
        copy.start()
    for copy in small[:4]:
        copy.wait()
    size, nodes = expand_in.shape
    rows = size // nodes
    expand = expand_in[...]
    same = lax.broadcasted_iota(jnp.int32, (size, size), 0) % rows
    same = same == lax.broadcasted_iota(jnp.int32, (size, size), 1) % rows
    own = lax.broadcasted_iota(jnp.int32, (nodes, size), 1) % rows == 0
    for d in range(3):
        wide = lax.dot_general(
            deriv_in[d], expand, (((1,), (1,)), ((), ())), preferred_element_type=f32
        ).astype(bf16)
        both = jnp.dot(expand, wide, preferred_element_type=f32)
        full_ref[:, d * size : (d + 1) * size] = jnp.where(same, both, 0.0).astype(bf16)
        first_ref[:, d * size : (d + 1) * size] = jnp.where(own, wide.astype(f32), 0.0).astype(bf16)
    full_ref[:, 3 * size :] = jump_in[:size]
    first_ref[:, 3 * size :] = jump_in[size:]
    block_ref[...] = jnp.zeros_like(block_ref)
    high, low = split(stiff_in[...])
    for v in range(block_ref.shape[1] // nodes):
        at = slice(v * nodes, (v + 1) * nodes)
        block_ref[0, at, at] = high
        block_ref[1, at, at] = low
    for copy in small[4:-1] + large + small[-1:]:
        copy.wait()


def fill_columns(stack_ref, speed_ref, own_at, last_at, edge_at, top_at, comps):
    size, width = speed_ref.shape[1:]
    face = size // Q
    for d in range(3):
        speed_ref[d] = advection[d] + own_at(1 + d).astype(f32)
    lane = lax.broadcasted_iota(jnp.int32, (face, width), 1)
    for v in range(comps):
        own = own_at(v)
        wide = own.astype(f32)
        for d in range(3):
            stack_ref[d * size : (d + 1) * size] = (wide * speed_ref[d]).astype(bf16)
        stack_ref[3 * size : 4 * size] = own
        last = pltpu.roll(last_at(v).astype(f32), 1, 1)
        edge = pltpu.roll(edge_at(v).astype(f32), 1, 1)
        edge = jnp.concatenate([edge] * (width // LANES), axis=1)
        stack_ref[4 * size : 4 * size + face] = jnp.where(lane == 0, edge, last).astype(bf16)
        stack_ref[4 * size + face :] = top_at(v)
        yield v


def outer_piece(tiles, edge, top, full, after, result, start, stop, width):
    count, comps, faces, _, rows, _ = tiles.shape
    size = faces * Q * rows
    face = faces * rows
    per_step = width // LANES
    held = (stop - start) * per_step
    shape = (comps, faces, Q, count, rows, LANES)

    def kernel(tiles_ref, edge_ref, top_ref, full_ref, *refs):
        out_ref, done_ref, stack_ref, speed_ref, held_ref, sem = refs[-6:]
        done_ref[...] = jnp.zeros_like(done_ref)

        def joined(read, height):
            return jnp.concatenate([read(k).reshape(height, LANES) for k in range(per_step)], axis=1)

        def copy(i):
            return pltpu.make_async_copy(
                held_ref.at[i], out_ref.at[:, :, :, start * per_step + i], sem.at[i]
            )

        def step(n, carry):
            base = (start + n) * per_step
            columns = fill_columns(
                stack_ref, speed_ref,
                lambda v: joined(lambda k: tiles_ref[base + k, v], size),
                lambda v: joined(lambda k: tiles_ref[base + k, v, :, Q - 1], face),
                lambda v: jnp.where(
                    base == 0,
                    edge_ref[v].reshape(face, LANES).astype(f32),
                    tiles_ref[jnp.maximum(base - 1, 0), v, :, Q - 1].reshape(face, LANES).astype(f32),
                ),
                lambda v: joined(lambda k: top_ref[base + k, v], face),
                comps,
            )
            for v in columns:
                value = jnp.dot(full_ref[...], stack_ref[...], preferred_element_type=f32).astype(bf16)
                for k in range(per_step):
                    part = value[:, k * LANES : (k + 1) * LANES].reshape(faces, Q, rows, LANES)
                    held_ref[n * per_step + k, v] = part
            for k in range(per_step):
                copy(n * per_step + k).start()
            return carry

        lax.fori_loop(0, stop - start, step, 0)
        for i in range(held):
            copy(i).wait()

    operands = [tiles, edge, top, full, after]
    specs = [in_vmem] * 5
    aliases = {}
    if result is not None:
        operands.append(held_in_hbm(result))
        specs.append(in_hbm)
        aliases = {5: 0}
    return pl.pallas_call(
        kernel,
        in_specs=specs,
        out_specs=[in_hbm, in_vmem],
        out_shape=[pltpu.HBM(shape, bf16), jax.ShapeDtypeStruct((8, LANES), f32)],
        scratch_shapes=[
            pltpu.VMEM((full.shape[1], width), bf16),
            pltpu.VMEM((3, size, width), f32),
            pltpu.VMEM((held, comps, faces, Q, rows, LANES), bf16),
            pltpu.SemaphoreType.DMA((held,)),
        ],
        input_output_aliases=aliases,
        compiler_params=params,
        name="outer",
    )(*operands)


def split(value):
    high = value.astype(bf16)
    return high, (value - high.astype(f32)).astype(bf16)


def whole(reduce, value):
    return reduce(reduce(value, axis=0, keepdims=True), axis=1, keepdims=True)


def rescale(value):
    top = whole(jnp.max, jnp.abs(value))
    by = jnp.where(top > 0.0, jnp.ceil(jnp.log2(jnp.maximum(top, 1e-37))), 0.0)
    return value * jnp.exp2(-by), by


def apply_blocks(count, value_ref, blocks_ref, out_ref):
    _, order = value_ref.shape
    rows = lax.broadcasted_iota(jnp.int32, (2 * GROUP, order), 0)
    out_ref[...] = jnp.zeros_like(out_ref)

    def group(g, carry):
        base = pl.multiple_of(g * GROUP, GROUP)
        terms = jnp.concatenate(split(value_ref[pl.ds(base, GROUP), :]), axis=0)
        kept = jnp.zeros((2 * GROUP, order), f32)
        for s in range(GROUP):
            product = lax.dot_general(
                terms, blocks_ref[base + s], (((1,), (1,)), ((), ())), preferred_element_type=f32
            )
            kept = jnp.where((rows == s) | (rows == s + GROUP), product, kept)
        out_ref[pl.ds(base, GROUP), :] = kept[:GROUP] + kept[GROUP:]
        return carry

    lax.fori_loop(0, (count + GROUP - 1) // GROUP, group, 0)


def emit(direction_ref, exponent, sent_ref, exponent_ref):
    slots, order = direction_ref.shape
    exponent_ref[...] = jnp.broadcast_to(exponent, exponent_ref.shape)
    sent_ref[:, :order] = direction_ref[...].astype(bf16)
    sent_ref[:, order:] = jnp.broadcast_to(exponent, (slots, sent_ref.shape[1] - order)).astype(bf16)


def live_rows(count, shape):
    return (lax.broadcasted_iota(jnp.int32, shape, 0) < count).astype(f32)


def start_kernel(
    count_ref, tiles_ref, edge_ref, corner_ref, first_ref, rhs_ref, blocks_ref,
    basis_ref, direction_ref, sent_ref, exponent_ref, stack_ref, speed_ref, trace_ref,
):
    slots, order = rhs_ref.shape
    _, comps, faces, _, rows, _ = tiles_ref.shape
    nodes = order // comps
    size, face = nodes * rows, faces * rows
    columns = fill_columns(
        stack_ref, speed_ref,
        lambda v: tiles_ref[0, v].reshape(size, LANES),
        lambda v: tiles_ref[0, v, :, Q - 1].reshape(face, LANES),
        lambda v: edge_ref[v].reshape(face, LANES),
        lambda v: corner_ref[v].reshape(face, LANES),
        comps,
    )
    for v in columns:
        value = jnp.dot(first_ref[...], stack_ref[...], preferred_element_type=f32)
        trace_ref[:, v * nodes : (v + 1) * nodes] = value.T[:slots]
    count = count_ref[0, 0]
    rhs = live_rows(count, rhs_ref.shape) * (rhs_ref[...] + time_step * trace_ref[...])
    basis, exponent = rescale(rhs)
    basis_ref[...] = basis
    apply_blocks(count, basis_ref, blocks_ref, direction_ref)
    emit(direction_ref, exponent, sent_ref, exponent_ref)


def operate(count_ref, direction_ref, exponent_ref, one_ref, two_ref, sigma_ref, stiff_ref):
    slots, order = direction_ref.shape
    direction = direction_ref[...]
    high, low = split(direction)
    both = jnp.dot(jnp.concatenate([high, low], axis=0), stiff_ref[0], preferred_element_type=f32)
    stiff = both[:slots] + both[slots:] + jnp.dot(high, stiff_ref[1], preferred_element_type=f32)
    exponent = exponent_ref[0:1, 0:1]
    exponent_one = jnp.max(one_ref[0:1, order:].astype(f32), axis=1, keepdims=True)
    exponent_two = jnp.max(two_ref[0:1, order:].astype(f32), axis=1, keepdims=True)
    common = jnp.maximum(exponent, jnp.maximum(exponent_one, exponent_two))
    own = direction + time_step * (sigma_ref[...] * direction + stiff)
    one = one_ref[:, :order].astype(f32) * jnp.exp2(exponent_one - common)
    two = two_ref[:, :order].astype(f32) * jnp.exp2(exponent_two - common)
    image = own * jnp.exp2(exponent - common) - coupling * (one + two)
    basis, by = rescale(live_rows(count_ref[0, 0], image.shape) * image)
    return basis, common + by


def middle_kernel(
    count_ref, previous_ref, previous_exponent_ref, one_ref, two_ref, sigma_ref, stiff_ref, blocks_ref, _,
    basis_ref, direction_ref, sent_ref, exponent_ref,
):
    basis, exponent = operate(
        count_ref, previous_ref, previous_exponent_ref, one_ref, two_ref, sigma_ref, stiff_ref
    )
    basis_ref[...] = basis
    apply_blocks(count_ref[0, 0], basis_ref, blocks_ref, direction_ref)
    emit(direction_ref, exponent, sent_ref, exponent_ref)


def pairs():
    return [(k, l) for k in range(ITERS + 1) for l in range(k, ITERS + 1)]


def gram_kernel(count_ref, _, previous_ref, *refs):
    exponent_refs, refs = refs[:ITERS], refs[ITERS:]
    one_ref, two_ref, sigma_ref, stiff_ref = refs[:4]
    basis_refs, part_ref = refs[4:-1], refs[-1]
    last, exponent = operate(
        count_ref, previous_ref, exponent_refs[-1], one_ref, two_ref, sigma_ref, stiff_ref
    )
    basis = [ref[...] for ref in basis_refs] + [last]
    lane = lax.broadcasted_iota(jnp.int32, (1, LANES), 1)
    row = jnp.zeros((1, LANES), f32)
    values = [whole(jnp.sum, basis[k] * basis[l]) for k, l in pairs()]
    values += [ref[0:1, 0:1] for ref in exponent_refs] + [exponent]
    for at, value in enumerate(values):
        row = jnp.where(lane == at, value, row)
    part_ref[...] = jnp.broadcast_to(row[None], part_ref.shape)


def finish_kernel(parts_ref, *refs):
    exponent_refs, direction_refs, out_ref = refs[:ITERS], refs[ITERS:-1], refs[-1]
    parts = parts_ref[:, 0, :]
    index = {pair: at for at, pair in enumerate(pairs())}
    count = ITERS + 1
    exponents = [parts[:, len(index) + k : len(index) + k + 1] for k in range(count)]
    tops = [jnp.max(e, axis=0, keepdims=True) for e in exponents]
    factors = [jnp.exp2(e - top) for e, top in zip(exponents, tops)]
    gram = {
        (k, l): jnp.sum(parts[:, at : at + 1] * factors[k] * factors[l], axis=0, keepdims=True)
        for (k, l), at in index.items()
    }
    scale = [lax.rsqrt(jnp.maximum(gram[k, k], 1e-37)) for k in range(count)]
    matrix = {(k, l): gram[k, l] * scale[k] * scale[l] for k, l in index}
    lower, inverse, middle = {}, [], []
    for k in range(ITERS):
        pivot = matrix[k + 1, k + 1]
        right = matrix[0, k + 1]
        for p in range(k):
            pivot = pivot - lower[k, p] * lower[k, p]
            right = right - lower[k, p] * middle[p]
        inverse.append(jnp.where(pivot > 5e-7, lax.rsqrt(jnp.maximum(pivot, 5e-7)), 0.0))
        for l in range(k + 1, ITERS):
            value = matrix[k + 1, l + 1]
            for p in range(k):
                value = value - lower[l, p] * lower[k, p]
            lower[l, k] = value * inverse[k]
        middle.append(right * inverse[k])
    weights = [None] * ITERS
    for k in reversed(range(ITERS)):
        value = middle[k]
        for l in range(k + 1, ITERS):
            value = value - lower[l, k] * weights[l]
        weights[k] = value * inverse[k]
    norm = gram[0, 0] * scale[0]
    total = None
    for k in range(ITERS):
        shift = jnp.exp2(tops[0] - tops[k + 1] + exponent_refs[k][0:1, 0:1])
        term = (weights[k] * scale[k + 1] * norm * shift) * direction_refs[k][...]
        total = term if total is None else total + term
    out_ref[...] = total


def per_device(outer_state, derivative, stiffness, wall_rhs, wall_sigma, wall_inverse, wall_count):
    comps, nodes, rows, cols = outer_state.shape
    slots, order = wall_rhs.shape
    faces = nodes // Q
    size = nodes * rows
    state = held_in_hbm(tile_view(outer_state.reshape(comps, faces, Q, rows, cols)))
    count = cols // LANES
    edge_shape = jax.ShapeDtypeStruct((comps, faces, rows, LANES), bf16)
    corner_shape = jax.ShapeDtypeStruct((comps, Q, Q, rows, LANES), bf16)

    edge, corner, top = pl.pallas_call(
        faces_kernel,
        in_specs=[in_hbm],
        out_specs=[in_vmem] * 3,
        out_shape=[edge_shape, corner_shape, jax.ShapeDtypeStruct((count, *corner_shape.shape), bf16)],
        scratch_shapes=[pltpu.SemaphoreType.DMA((2 + Q + count * Q,))],
        compiler_params=params,
        name="faces",
    )(state)
    came_edge = lax.ppermute(edge, "gx", ring("gx", 1))
    came_corner = from_below(corner, "gy")
    came_top = from_below(top, "gy")

    jumps = jump_matrix(nodes, rows)
    depth = 3 * size + jumps.shape[1]
    expand = np.repeat(np.eye(nodes, dtype=np.float32), rows, axis=0)
    jumps = np.concatenate([jumps, jumps[::rows]])
    operands = (
        state, wall_inverse, wall_rhs, wall_sigma, derivative, stiffness, jnp.asarray(expand, bf16),
        jnp.asarray(jumps, bf16),
    )
    operands = tuple(held_in_hbm(operand) for operand in operands)
    tiles, blocks, rhs, sigma, full, first, stiff = pl.pallas_call(
        prep_kernel,
        in_specs=[in_hbm] * len(operands),
        out_specs=[in_vmem] * 7,
        out_shape=[
            jax.ShapeDtypeStruct((count, comps, faces, Q, rows, LANES), bf16),
            jax.ShapeDtypeStruct(wall_inverse.shape, bf16),
            jax.ShapeDtypeStruct(wall_rhs.shape, f32),
            jax.ShapeDtypeStruct(wall_sigma.shape, f32),
            jax.ShapeDtypeStruct((size, depth), bf16),
            jax.ShapeDtypeStruct((nodes, depth), bf16),
            jax.ShapeDtypeStruct((2, order, order), bf16),
        ],
        scratch_shapes=[pltpu.VMEM(a.shape, a.dtype) for a in (derivative, stiffness)]
        + [pltpu.VMEM(expand.shape, bf16), pltpu.VMEM(jumps.shape, bf16), pltpu.SemaphoreType.DMA((7 + count,))],
        compiler_params=params,
        name="prep",
    )(*operands)

    vector = jax.ShapeDtypeStruct((slots, order), f32)
    padded = -(-(order + 1) // LANES) * LANES
    step_shapes = [
        vector, vector, jax.ShapeDtypeStruct((slots, padded), bf16), jax.ShapeDtypeStruct((8, LANES), f32),
    ]
    basis, direction, sent, exponent = pl.pallas_call(
        start_kernel,
        in_specs=[in_smem] + [in_vmem] * 6,
        out_specs=[in_vmem] * 4,
        out_shape=step_shapes,
        scratch_shapes=[
            pltpu.VMEM((depth, LANES), bf16), pltpu.VMEM((3, size, LANES), f32), pltpu.VMEM((slots, order), f32),
        ],
        compiler_params=params,
        name="start",
    )(wall_count, tiles, came_edge, came_corner, first, rhs, blocks)
    bases, directions, exponents = [basis], [direction], [exponent]

    width = 2 * LANES
    steps = cols // width
    bounds = [steps * k // ITERS for k in range(ITERS + 1)]
    residual = None
    for k in range(ITERS):
        one, two = neighbours(sent, "gx")
        residual, done = outer_piece(
            tiles, came_edge, came_top, full, exponent, residual, bounds[k], bounds[k + 1], width
        )
        if k < ITERS - 1:
            basis, direction, sent, exponent = pl.pallas_call(
                middle_kernel,
                in_specs=[in_smem] + [in_vmem] * 8,
                out_specs=[in_vmem] * 4,
                out_shape=step_shapes,
                compiler_params=params,
                name="middle",
            )(wall_count, direction, exponent, one, two, sigma, stiff, blocks, done)
            bases.append(basis)
            directions.append(direction)
            exponents.append(exponent)

    devices = lax.axis_size("gx") * lax.axis_size("gy")
    part = pl.pallas_call(
        gram_kernel,
        in_specs=[in_smem] + [in_vmem] * (6 + 2 * ITERS),
        out_specs=in_vmem,
        out_shape=jax.ShapeDtypeStruct((devices, 1, LANES), f32),
        compiler_params=params,
        name="gram",
    )(wall_count, done, direction, *exponents, one, two, sigma, stiff, *bases)
    parts = lax.all_to_all(part, ("gx", "gy"), 0, 0)
    wall_update = pl.pallas_call(
        finish_kernel,
        in_specs=[in_vmem] * (1 + 2 * ITERS),
        out_specs=in_vmem,
        out_shape=vector,
        compiler_params=params,
        name="finish",
    )(parts, *exponents, *directions)
    return from_tile_view(residual).reshape(outer_state.shape), wall_update


def solution(mesh):
    in_specs = (
        P(None, None, "gy", "gx"),
        P(),
        P(),
        P(("gx", "gy"), None),
        P(("gx", "gy"), None),
        P(("gx", "gy"), None, None),
        P("gx", "gy"),
    )
    out_specs = (P(None, None, "gy", "gx"), P(("gx", "gy"), None))
    return jax.shard_map(
        per_device, mesh=mesh, in_specs=in_specs, out_specs=out_specs, check_vma=False
    )
```

```python
import jax
import jax.numpy as jnp
import numpy as np
from jax import lax
from jax.experimental import pallas as pl
from jax.experimental.pallas import tpu as pltpu
from jax.sharding import PartitionSpec as P


Q = 4
ITERS = 3

time_step = 0.3
coupling = 0.25
upwind_x = 2.0
upwind_y = 1.0
advection = (1.0, 0.5, 0.25)

LANES = 128
GROUP = 8
PRICE = 16 << 20
VMEM_BYTES = 24 << 20
bf16 = jnp.bfloat16
f32 = jnp.float32

in_vmem = pl.BlockSpec(memory_space=pltpu.VMEM)
in_smem = pl.BlockSpec(memory_space=pltpu.SMEM)
in_hbm = pl.BlockSpec(memory_space=pltpu.HBM)
params = pltpu.CompilerParams(vmem_limit_bytes=VMEM_BYTES)


def held_in_hbm(array):
    return pltpu.with_memory_space_constraint(array, pltpu.HBM)


def ring(axis, by):
    count = lax.axis_size(axis)
    return [(i, (i + by) % count) for i in range(count)]


def neighbours(array, axis):
    count = lax.axis_size(axis)
    if count % 2 or count < 4:
        return lax.ppermute(array, axis, ring(axis, 1)), lax.ppermute(array, axis, ring(axis, -1))
    even = [(i, i ^ 1) for i in range(count)]
    odd = [(i, (i + (1 if i % 2 else -1)) % count) for i in range(count)]
    return lax.ppermute(array, axis, even), lax.ppermute(array, axis, odd)


def jump_matrix(nodes, rows):
    faces = nodes // Q
    out = np.zeros((nodes * rows, nodes * rows + 2 * faces * rows), np.float32)
    for m in range(nodes):
        i, j, k = m % Q, m // Q % Q, m // (Q * Q)
        for r in range(rows):
            row = m * rows + r
            if i == 0:
                out[row, row] -= upwind_x
                out[row, nodes * rows + (m // Q) * rows + r] += upwind_x
            if j == 0:
                out[row, row] -= upwind_y
                if r > 0:
                    out[row, (m + Q * (Q - 1)) * rows + r - 1] += upwind_y
                else:
                    column = (k * Q + i) * rows + rows - 1
                    out[row, (nodes + faces) * rows + column] += upwind_y
    return out


def tile_view(array):
    *lead, rows, cols = array.shape
    return jnp.swapaxes(array.reshape(*lead, rows, cols // LANES, LANES), -3, -2)


def from_tile_view(array):
    *lead, tiles, rows, lanes = array.shape
    return jnp.swapaxes(array, -3, -2).reshape(*lead, rows, tiles * lanes)


def top_row(state_ref, t, k, target_ref, sem):
    return pltpu.make_async_copy(state_ref.at[:, pl.ds(k * Q + Q - 1, 1), :, t], target_ref.at[:, pl.ds(k, 1)], sem)


def faces_kernel(state_ref, edge_ref, corner_ref, sem):
    tiles = state_ref.shape[3]
    copies = [top_row(state_ref, 0, k, corner_ref, sem.at[k]) for k in range(Q)]
    copies.append(pltpu.make_async_copy(state_ref.at[:, :, Q - 1, tiles - 1], edge_ref, sem.at[Q]))
    for copy in copies:
        copy.start()
    for copy in copies:
        copy.wait()


def prep_kernel(
    state_ref, rhs_ref, sigma_ref, deriv_ref, stiff_ref, expand_ref, jump_ref,
    top_ref, tile_ref, rhs_out_ref, sigma_out_ref, full_ref, first_ref, block_ref,
    deriv_in, stiff_in, expand_in, jump_in, sem,
):
    count = top_ref.shape[0]
    pairs_of_refs = [
        (deriv_ref, deriv_in), (expand_ref, expand_in), (jump_ref, jump_in), (stiff_ref, stiff_in),
        (state_ref.at[:, :, :, 0], tile_ref), (rhs_ref, rhs_out_ref), (sigma_ref, sigma_out_ref),
    ]
    copies = [pltpu.make_async_copy(a, b, sem.at[at]) for at, (a, b) in enumerate(pairs_of_refs)]
    copies += [
        top_row(state_ref, t, k, top_ref.at[t], sem.at[len(pairs_of_refs) + t * Q + k])
        for t in range(count)
        for k in range(Q)
    ]
    for copy in copies:
        copy.start()
    for copy in copies[:4]:
        copy.wait()
    size, nodes = expand_in.shape
    rows = size // nodes
    expand = expand_in[...]
    same = lax.broadcasted_iota(jnp.int32, (size, size), 0) % rows
    same = same == lax.broadcasted_iota(jnp.int32, (size, size), 1) % rows
    own = lax.broadcasted_iota(jnp.int32, (nodes, size), 1) % rows == 0
    for d in range(3):
        wide = lax.dot_general(
            deriv_in[d], expand, (((1,), (1,)), ((), ())), preferred_element_type=f32
        ).astype(bf16)
        both = jnp.dot(expand, wide, preferred_element_type=f32)
        full_ref[:, d * size : (d + 1) * size] = jnp.where(same, both, 0.0).astype(bf16)
        first_ref[:, d * size : (d + 1) * size] = jnp.where(own, wide.astype(f32), 0.0).astype(bf16)
    jump = jump_in[...]
    below = lax.broadcasted_iota(jnp.int32, jump.shape, 1) >= jump.shape[1] - size // Q
    jump = jnp.where(below & (lax.axis_index("gy") == 0), 0.0, jump.astype(f32)).astype(bf16)
    full_ref[:, 3 * size :] = jump[:size]
    first_ref[:, 3 * size :] = jump[size:]
    block_ref[...] = jnp.zeros_like(block_ref)
    high, low = split(stiff_in[...])
    for v in range(block_ref.shape[1] // nodes):
        at = slice(v * nodes, (v + 1) * nodes)
        block_ref[0, at, at] = high
        block_ref[1, at, at] = low
    for copy in copies[4:]:
        copy.wait()


def fill_columns(stack_ref, speed_ref, own_at, last_at, edge_at, top_at, comps):
    size, width = speed_ref.shape[1:]
    face = size // Q
    for d in range(3):
        speed_ref[d] = advection[d] + own_at(1 + d).astype(f32)
    lane = lax.broadcasted_iota(jnp.int32, (face, width), 1)
    for v in range(comps):
        own = own_at(v)
        wide = own.astype(f32)
        for d in range(3):
            stack_ref[d * size : (d + 1) * size] = (wide * speed_ref[d]).astype(bf16)
        stack_ref[3 * size : 4 * size] = own
        last = pltpu.roll(last_at(v).astype(f32), 1, 1)
        edge = pltpu.roll(edge_at(v).astype(f32), 1, 1)
        edge = jnp.concatenate([edge] * (width // LANES), axis=1)
        stack_ref[4 * size : 4 * size + face] = jnp.where(lane == 0, edge, last).astype(bf16)
        stack_ref[4 * size + face :] = top_at(v)
        yield v


def outer_piece(tiles, edge, top, full, after, result, start, stop, width):
    count, comps, faces, _, rows, _ = tiles.shape
    size = faces * Q * rows
    face = faces * rows
    per_step = width // LANES
    held = (stop - start) * per_step
    shape = (comps, faces, Q, count, rows, LANES)

    def kernel(tiles_ref, edge_ref, top_ref, full_ref, *refs):
        out_ref, done_ref, stack_ref, speed_ref, held_ref, sem = refs[-6:]
        done_ref[...] = jnp.zeros_like(done_ref)

        def joined(read, height):
            return jnp.concatenate([read(k).reshape(height, LANES) for k in range(per_step)], axis=1)

        def copy(i):
            return pltpu.make_async_copy(
                held_ref.at[i], out_ref.at[:, :, :, start * per_step + i], sem.at[i]
            )

        def step(n, carry):
            base = (start + n) * per_step
            columns = fill_columns(
                stack_ref, speed_ref,
                lambda v: joined(lambda k: tiles_ref[base + k, v], size),
                lambda v: joined(lambda k: tiles_ref[base + k, v, :, Q - 1], face),
                lambda v: jnp.where(
                    base == 0,
                    edge_ref[v].reshape(face, LANES).astype(f32),
                    tiles_ref[jnp.maximum(base - 1, 0), v, :, Q - 1].reshape(face, LANES).astype(f32),
                ),
                lambda v: joined(lambda k: top_ref[base + k, v], face),
                comps,
            )
            for v in columns:
                value = jnp.dot(full_ref[...], stack_ref[...], preferred_element_type=f32).astype(bf16)
                for k in range(per_step):
                    part = value[:, k * LANES : (k + 1) * LANES].reshape(faces, Q, rows, LANES)
                    held_ref[n * per_step + k, v] = part
            for k in range(per_step):
                copy(n * per_step + k).start()
            return carry

        lax.fori_loop(0, stop - start, step, 0)
        for i in range(held):
            copy(i).wait()

    operands = [tiles, edge, top, full, after]
    specs = [in_vmem] * 5
    aliases = {}
    if result is not None:
        operands.append(held_in_hbm(result))
        specs.append(in_hbm)
        aliases = {5: 0}
    return pl.pallas_call(
        kernel,
        in_specs=specs,
        out_specs=[in_hbm, in_vmem],
        out_shape=[pltpu.HBM(shape, bf16), jax.ShapeDtypeStruct((8, LANES), f32)],
        scratch_shapes=[
            pltpu.VMEM((full.shape[1], width), bf16),
            pltpu.VMEM((3, size, width), f32),
            pltpu.VMEM((held, comps, faces, Q, rows, LANES), bf16),
            pltpu.SemaphoreType.DMA((held,)),
        ],
        input_output_aliases=aliases,
        compiler_params=params,
        name="outer",
    )(*operands)


def split(value):
    high = value.astype(bf16)
    return high, (value - high.astype(f32)).astype(bf16)


def whole(reduce, value):
    return reduce(reduce(value, axis=0, keepdims=True), axis=1, keepdims=True)


def rescale(value):
    top = whole(jnp.max, jnp.abs(value))
    by = jnp.where(top > 0.0, jnp.ceil(jnp.log2(jnp.maximum(top, 1e-37))), 0.0)
    return value * jnp.exp2(-by), by


def group_count(count):
    return (count + GROUP - 1) // GROUP


def apply_blocks(count, value_ref, block_at, out_ref):
    _, order = value_ref.shape
    rows = lax.broadcasted_iota(jnp.int32, (2 * GROUP, order), 0)
    out_ref[...] = jnp.zeros_like(out_ref)

    def group(g, carry):
        base = pl.multiple_of(g * GROUP, GROUP)
        block = block_at(g)
        terms = jnp.concatenate(split(value_ref[pl.ds(base, GROUP), :]), axis=0)
        kept = jnp.zeros((2 * GROUP, order), f32)
        for s in range(GROUP):
            product = jnp.dot(terms, block(base + s), preferred_element_type=f32)
            kept = jnp.where((rows == s) | (rows == s + GROUP), product, kept)
        out_ref[pl.ds(base, GROUP), :] = kept[:GROUP] + kept[GROUP:]
        return carry

    lax.fori_loop(0, group_count(count), group, 0)


def emit(direction_ref, exponent, sent_ref, exponent_ref):
    slots, order = direction_ref.shape
    exponent_ref[...] = jnp.broadcast_to(exponent, exponent_ref.shape)
    sent_ref[:, :order] = direction_ref[...].astype(bf16)
    sent_ref[:, order:] = jnp.broadcast_to(exponent, (slots, sent_ref.shape[1] - order)).astype(bf16)


def live_rows(count, shape):
    return (lax.broadcasted_iota(jnp.int32, shape, 0) < count).astype(f32)


def start_kernel(
    count_ref, state_ref, blocks_in_ref, tile_ref, edge_ref, corner_ref, first_ref, rhs_ref,
    basis_ref, direction_ref, sent_ref, exponent_ref, tiles_ref, blocks_ref,
    stack_ref, speed_ref, trace_ref, stage_ref, tile_sem, block_sem,
):
    slots, order = rhs_ref.shape
    tiles, comps, faces, _, rows, _ = tiles_ref.shape
    count = count_ref[0, 0]

    def tile_copy(t):
        return pltpu.make_async_copy(state_ref.at[:, :, :, t], tiles_ref.at[t], tile_sem.at[t])

    def block_copy(g):
        part = pl.ds(g * GROUP, GROUP)
        return pltpu.make_async_copy(blocks_in_ref.at[part], stage_ref.at[part], block_sem.at[g])

    def arrived(g):
        block_copy(g).wait()

        def block(at):
            turned = stage_ref[at].T
            blocks_ref[at] = turned
            return turned

        return block

    for g in range(slots // GROUP):
        pl.when(g < group_count(count))(block_copy(g).start)
    for t in range(tiles):
        tile_copy(t).start()
    nodes = order // comps
    size, face = nodes * rows, faces * rows
    columns = fill_columns(
        stack_ref, speed_ref,
        lambda v: tile_ref[v].reshape(size, LANES),
        lambda v: tile_ref[v, :, Q - 1].reshape(face, LANES),
        lambda v: edge_ref[v].reshape(face, LANES),
        lambda v: corner_ref[v].reshape(face, LANES),
        comps,
    )
    for v in columns:
        value = jnp.dot(first_ref[...], stack_ref[...], preferred_element_type=f32)
        trace_ref[:, v * nodes : (v + 1) * nodes] = value.T[:slots]
    rhs = live_rows(count, rhs_ref.shape) * (rhs_ref[...] + time_step * trace_ref[...])
    basis, exponent = rescale(rhs)
    basis_ref[...] = basis
    apply_blocks(count, basis_ref, arrived, direction_ref)
    emit(direction_ref, exponent, sent_ref, exponent_ref)
    for t in range(tiles):
        tile_copy(t).wait()


def operate(count_ref, direction_ref, exponent_ref, one_ref, two_ref, sigma_ref, stiff_ref):
    slots, order = direction_ref.shape
    direction = direction_ref[...]
    high, low = split(direction)
    both = jnp.dot(jnp.concatenate([high, low], axis=0), stiff_ref[0], preferred_element_type=f32)
    stiff = both[:slots] + both[slots:] + jnp.dot(high, stiff_ref[1], preferred_element_type=f32)
    exponent = exponent_ref[0:1, 0:1]
    exponent_one = jnp.max(one_ref[0:1, order:].astype(f32), axis=1, keepdims=True)
    exponent_two = jnp.max(two_ref[0:1, order:].astype(f32), axis=1, keepdims=True)
    common = jnp.maximum(exponent, jnp.maximum(exponent_one, exponent_two))
    own = direction + time_step * (sigma_ref[...] * direction + stiff)
    one = one_ref[:, :order].astype(f32) * jnp.exp2(exponent_one - common)
    two = two_ref[:, :order].astype(f32) * jnp.exp2(exponent_two - common)
    image = own * jnp.exp2(exponent - common) - coupling * (one + two)
    basis, by = rescale(live_rows(count_ref[0, 0], image.shape) * image)
    return basis, common + by


def middle_kernel(
    count_ref, previous_ref, previous_exponent_ref, one_ref, two_ref, sigma_ref, stiff_ref, blocks_ref, _,
    basis_ref, direction_ref, sent_ref, exponent_ref,
):
    basis, exponent = operate(
        count_ref, previous_ref, previous_exponent_ref, one_ref, two_ref, sigma_ref, stiff_ref
    )
    basis_ref[...] = basis
    apply_blocks(count_ref[0, 0], basis_ref, lambda g: lambda at: blocks_ref[at], direction_ref)
    emit(direction_ref, exponent, sent_ref, exponent_ref)


def pairs():
    return [(k, l) for k in range(ITERS + 1) for l in range(k, ITERS + 1)]


def gram_kernel(count_ref, _, previous_ref, *refs):
    exponent_refs, refs = refs[:ITERS], refs[ITERS:]
    one_ref, two_ref, sigma_ref, stiff_ref = refs[:4]
    basis_refs, part_ref = refs[4:-1], refs[-1]
    last, exponent = operate(
        count_ref, previous_ref, exponent_refs[-1], one_ref, two_ref, sigma_ref, stiff_ref
    )
    basis = [ref[...] for ref in basis_refs] + [last]
    lane = lax.broadcasted_iota(jnp.int32, (1, LANES), 1)
    row = jnp.zeros((1, LANES), f32)
    values = [whole(jnp.sum, basis[k] * basis[l]) for k, l in pairs()]
    values += [ref[0:1, 0:1] for ref in exponent_refs] + [exponent]
    for at, value in enumerate(values):
        row = jnp.where(lane == at, value, row)
    part_ref[...] = jnp.broadcast_to(row[None], part_ref.shape)


def finish_kernel(parts_ref, *refs):
    exponent_refs, direction_refs, out_ref = refs[:ITERS], refs[ITERS:-1], refs[-1]
    parts = parts_ref[:, 0, :]
    index = {pair: at for at, pair in enumerate(pairs())}
    count = ITERS + 1
    exponents = [parts[:, len(index) + k : len(index) + k + 1] for k in range(count)]
    tops = [jnp.max(e, axis=0, keepdims=True) for e in exponents]
    factors = [jnp.exp2(e - top) for e, top in zip(exponents, tops)]
    gram = {
        (k, l): jnp.sum(parts[:, at : at + 1] * factors[k] * factors[l], axis=0, keepdims=True)
        for (k, l), at in index.items()
    }
    scale = [lax.rsqrt(jnp.maximum(gram[k, k], 1e-37)) for k in range(count)]
    matrix = {(k, l): gram[k, l] * scale[k] * scale[l] for k, l in index}
    lower, inverse, middle = {}, [], []
    for k in range(ITERS):
        pivot = matrix[k + 1, k + 1]
        right = matrix[0, k + 1]
        for p in range(k):
            pivot = pivot - lower[k, p] * lower[k, p]
            right = right - lower[k, p] * middle[p]
        inverse.append(jnp.where(pivot > 5e-7, lax.rsqrt(jnp.maximum(pivot, 5e-7)), 0.0))
        for l in range(k + 1, ITERS):
            value = matrix[k + 1, l + 1]
            for p in range(k):
                value = value - lower[l, p] * lower[k, p]
            lower[l, k] = value * inverse[k]
        middle.append(right * inverse[k])
    weights = [None] * ITERS
    for k in reversed(range(ITERS)):
        value = middle[k]
        for l in range(k + 1, ITERS):
            value = value - lower[l, k] * weights[l]
        weights[k] = value * inverse[k]
    norm = gram[0, 0] * scale[0]
    total = None
    for k in range(ITERS):
        shift = jnp.exp2(tops[0] - tops[k + 1] + exponent_refs[k][0:1, 0:1])
        term = (weights[k] * scale[k + 1] * norm * shift) * direction_refs[k][...]
        total = term if total is None else total + term
    out_ref[...] = total


def solve(outer_state, derivative, stiffness, wall_rhs, wall_sigma, wall_inverse, wall_count):
    comps, nodes, rows, cols = outer_state.shape
    slots, order = wall_rhs.shape
    faces = nodes // Q
    size = nodes * rows
    state = held_in_hbm(tile_view(outer_state.reshape(comps, faces, Q, rows, cols)))
    count = cols // LANES
    edge, corner = pl.pallas_call(
        faces_kernel,
        in_specs=[in_hbm],
        out_specs=[in_vmem] * 2,
        out_shape=[
            jax.ShapeDtypeStruct((comps, faces, rows, LANES), bf16),
            jax.ShapeDtypeStruct((comps, Q, Q, rows, LANES), bf16),
        ],
        scratch_shapes=[pltpu.SemaphoreType.DMA((Q + 1,))],
        compiler_params=params,
        cost_estimate=pl.CostEstimate(flops=0, transcendentals=0, bytes_accessed=PRICE),
        name="faces",
    )(state)
    came_corner = lax.ppermute(corner, "gy", ring("gy", 1))
    came_edge = lax.ppermute(edge, "gx", ring("gx", 1))

    jumps = jump_matrix(nodes, rows)
    depth = 3 * size + jumps.shape[1]
    expand = np.repeat(np.eye(nodes, dtype=np.float32), rows, axis=0)
    jumps = np.concatenate([jumps, jumps[::rows]])
    operands = (
        state, wall_rhs, wall_sigma, derivative, stiffness, jnp.asarray(expand, bf16),
        jnp.asarray(jumps, bf16),
    )
    operands = tuple(held_in_hbm(operand) for operand in operands)
    top, tile, rhs, sigma, full, first, stiff = pl.pallas_call(
        prep_kernel,
        in_specs=[in_hbm] * len(operands),
        out_specs=[in_vmem] * 7,
        out_shape=[
            jax.ShapeDtypeStruct((count, *corner.shape), bf16),
            jax.ShapeDtypeStruct((comps, faces, Q, rows, LANES), bf16),
            jax.ShapeDtypeStruct(wall_rhs.shape, f32),
            jax.ShapeDtypeStruct(wall_sigma.shape, f32),
            jax.ShapeDtypeStruct((size, depth), bf16),
            jax.ShapeDtypeStruct((nodes, depth), bf16),
            jax.ShapeDtypeStruct((2, order, order), bf16),
        ],
        scratch_shapes=[pltpu.VMEM(a.shape, a.dtype) for a in (derivative, stiffness)]
        + [pltpu.VMEM(expand.shape, bf16), pltpu.VMEM(jumps.shape, bf16)]
        + [pltpu.SemaphoreType.DMA((7 + count * Q,))],
        compiler_params=params,
        cost_estimate=pl.CostEstimate(flops=0, transcendentals=0, bytes_accessed=PRICE),
        name="prep",
    )(*operands)
    came_top = lax.ppermute(top, "gy", ring("gy", 1))

    vector = jax.ShapeDtypeStruct((slots, order), f32)
    padded = -(-(order + 1) // LANES) * LANES
    step_shapes = [
        vector, vector, jax.ShapeDtypeStruct((slots, padded), bf16), jax.ShapeDtypeStruct((8, LANES), f32),
    ]
    basis, direction, sent, exponent, tiles, blocks = pl.pallas_call(
        start_kernel,
        in_specs=[in_smem] + [in_hbm] * 2 + [in_vmem] * 5,
        out_specs=[in_vmem] * 6,
        out_shape=step_shapes + [
            jax.ShapeDtypeStruct((count, comps, faces, Q, rows, LANES), bf16),
            jax.ShapeDtypeStruct(wall_inverse.shape, bf16),
        ],
        scratch_shapes=[
            pltpu.VMEM((depth, LANES), bf16), pltpu.VMEM((3, size, LANES), f32), pltpu.VMEM((slots, order), f32),
            pltpu.VMEM(wall_inverse.shape, bf16),
            pltpu.SemaphoreType.DMA((count,)), pltpu.SemaphoreType.DMA((slots // GROUP,)),
        ],
        compiler_params=params,
        name="start",
    )(wall_count, state, held_in_hbm(wall_inverse), tile, came_edge, came_corner, first, rhs)
    bases, directions, exponents = [basis], [direction], [exponent]

    width = 2 * LANES
    steps = cols // width
    bounds = [steps * k // ITERS for k in range(ITERS + 1)]
    residual = None
    for k in range(ITERS):
        one, two = neighbours(sent, "gx")
        residual, done = outer_piece(
            tiles, came_edge, came_top, full, exponent, residual, bounds[k], bounds[k + 1], width
        )
        if k < ITERS - 1:
            basis, direction, sent, exponent = pl.pallas_call(
                middle_kernel,
                in_specs=[in_smem] + [in_vmem] * 8,
                out_specs=[in_vmem] * 4,
                out_shape=step_shapes,
                compiler_params=params,
                name="middle",
            )(wall_count, direction, exponent, one, two, sigma, stiff, blocks, done)
            bases.append(basis)
            directions.append(direction)
            exponents.append(exponent)

    devices = lax.axis_size("gx") * lax.axis_size("gy")
    part = pl.pallas_call(
        gram_kernel,
        in_specs=[in_smem] + [in_vmem] * (6 + 2 * ITERS),
        out_specs=in_vmem,
        out_shape=jax.ShapeDtypeStruct((devices, 1, LANES), f32),
        compiler_params=params,
        name="gram",
    )(wall_count, done, direction, *exponents, one, two, sigma, stiff, *bases)
    parts = lax.all_to_all(part, ("gx", "gy"), 0, 0)
    wall_update = pl.pallas_call(
        finish_kernel,
        in_specs=[in_vmem] * (1 + 2 * ITERS),
        out_specs=in_vmem,
        out_shape=vector,
        compiler_params=params,
        name="finish",
    )(parts, *exponents, *directions)
    return from_tile_view(residual).reshape(outer_state.shape), wall_update


def solution(mesh):
    in_specs = (
        P(None, None, "gy", "gx"),
        P(),
        P(),
        P(("gx", "gy"), None),
        P(("gx", "gy"), None),
        P(("gx", "gy"), None, None),
        P("gx", "gy"),
    )
    out_specs = (P(None, None, "gy", "gx"), P(("gx", "gy"), None))
    return jax.shard_map(solve, mesh=mesh, in_specs=in_specs, out_specs=out_specs, check_vma=False)
```

```python
import jax
import jax.numpy as jnp
import numpy as np
from jax import lax
from jax.experimental import pallas as pl
from jax.experimental.pallas import tpu as pltpu
from jax.sharding import PartitionSpec as P


Q = 4
ITERS = 3

time_step = 0.3
coupling = 0.25
upwind_x = 2.0
upwind_y = 1.0
advection = (1.0, 0.5, 0.25)

LANES = 128
GROUP = 16
VMEM_BYTES = 24 << 20
bf16 = jnp.bfloat16
f32 = jnp.float32

in_vmem = pl.BlockSpec(memory_space=pltpu.VMEM)
in_hbm = pl.BlockSpec(memory_space=pltpu.HBM)
params = pltpu.CompilerParams(vmem_limit_bytes=VMEM_BYTES)


def held_in_hbm(array):
    return pltpu.with_memory_space_constraint(array, pltpu.HBM)


def ring(axis, by):
    count = lax.axis_size(axis)
    return [(i, (i + by) % count) for i in range(count)]


def neighbours(array, axis):
    count = lax.axis_size(axis)
    if count % 2 or count < 4:
        first, second = ring(axis, 1), ring(axis, -1)
    else:
        first = [(i, i ^ 1) for i in range(count)]
        second = [(i, (i + (1 if i % 2 else -1)) % count) for i in range(count)]
    one = lax.ppermute(array, axis, first)
    two = lax.ppermute(array, axis, second)
    return one, two


def jump_matrix(nodes, rows):
    faces = nodes // Q
    out = np.zeros((nodes * rows, nodes * rows + 2 * faces * rows), np.float32)
    for m in range(nodes):
        i, j, k = m % Q, m // Q % Q, m // (Q * Q)
        for r in range(rows):
            row = m * rows + r
            if i == 0:
                out[row, row] -= upwind_x
                out[row, nodes * rows + (m // Q) * rows + r] += upwind_x
            if j == 0:
                out[row, row] -= upwind_y
                if r > 0:
                    out[row, (m + Q * (Q - 1)) * rows + r - 1] += upwind_y
                else:
                    column = (k * Q + i) * rows + rows - 1
                    out[row, (nodes + faces) * rows + column] += upwind_y
    return out


def tile_view(array):
    *lead, rows, cols = array.shape
    return jnp.swapaxes(array.reshape(*lead, rows, cols // LANES, LANES), -3, -2)


def from_tile_view(array):
    *lead, tiles, rows, lanes = array.shape
    return jnp.swapaxes(array, -3, -2).reshape(*lead, rows, tiles * lanes)


def faces_kernel(state_ref, edge_ref, corner_ref, sem):
    tiles = state_ref.shape[3]
    copies = [pltpu.make_async_copy(state_ref.at[:, :, Q - 1, tiles - 1], edge_ref, sem.at[0])]
    for k in range(Q):
        rows = state_ref.at[:, pl.ds(k * Q + Q - 1, 1)]
        copies.append(pltpu.make_async_copy(rows.at[:, :, :, 0], corner_ref.at[:, pl.ds(k, 1)], sem.at[1 + k]))
    for copy in copies:
        copy.start()
    for copy in copies:
        copy.wait()


def prep_kernel(
    state_ref, blocks_in_ref, rhs_ref, sigma_ref, deriv_ref, stiff_ref, expand_ref, jump_ref,
    trace_ref, sigma_out_ref, full_ref, first_ref, block_ref, low_ref, high_ref, blocks_ref,
    rhs_in, deriv_in, stiff_in, expand_in, jump_in, tile_ref, side_ref, stack_ref, speed_ref, copy_ref, sem,
):
    pairs_of_refs = [
        (deriv_ref, deriv_in), (expand_ref, expand_in), (jump_ref, jump_in), (stiff_ref, stiff_in),
        (state_ref.at[:, :, :, 0], tile_ref), (state_ref.at[:, :, Q - 1, 0], side_ref),
        (rhs_ref, rhs_in), (sigma_ref, sigma_out_ref),
    ]
    pairs_of_refs.append((blocks_in_ref.at[pl.ds(0, blocks_ref.shape[0])], blocks_ref))
    half = low_ref.shape[3]
    for k in range(Q):
        rows_at = state_ref.at[:, pl.ds(k * Q + Q - 1, 1)]
        pairs_of_refs.append((rows_at.at[:, :, :, pl.ds(0, half)], low_ref.at[:, pl.ds(k, 1)]))
        pairs_of_refs.append((rows_at.at[:, :, :, pl.ds(half, half)], high_ref.at[:, pl.ds(k, 1)]))
    copies = [pltpu.make_async_copy(a, b, sem.at[at]) for at, (a, b) in enumerate(pairs_of_refs)]
    for copy in copies:
        copy.start()
    for copy in copies[:4]:
        copy.wait()
    size, nodes = expand_in.shape
    rows = size // nodes
    expand = expand_in[...]
    same = lax.broadcasted_iota(jnp.int32, (size, size), 0) % rows
    same = same == lax.broadcasted_iota(jnp.int32, (size, size), 1) % rows
    own = lax.broadcasted_iota(jnp.int32, (nodes, size), 1) % rows == 0
    for d in range(3):
        wide = lax.dot_general(
            deriv_in[d], expand, (((1,), (1,)), ((), ())), preferred_element_type=f32
        ).astype(bf16)
        both = jnp.dot(expand, wide, preferred_element_type=f32)
        full_ref[:, d * size : (d + 1) * size] = jnp.where(same, both, 0.0).astype(bf16)
        first_ref[:, d * size : (d + 1) * size] = jnp.where(own, wide.astype(f32), 0.0).astype(bf16)
    jump = jump_in[...]
    below = lax.broadcasted_iota(jnp.int32, jump.shape, 1) >= jump.shape[1] - size // Q
    jump = jnp.where(below & (lax.axis_index("gy") == 0), 0.0, jump.astype(f32)).astype(bf16)
    full_ref[:, 3 * size :] = jump[:size]
    first_ref[:, 3 * size :] = jump[size:]
    block_ref[...] = jnp.zeros_like(block_ref)
    high, low = split(stiff_in[...])
    for v in range(block_ref.shape[1] // nodes):
        at = slice(v * nodes, (v + 1) * nodes)
        block_ref[0, at, at] = high
        block_ref[1, at, at] = low
    for copy in copies[4:8]:
        copy.wait()
    comps, faces, _, _, _ = tile_ref.shape
    face = faces * rows
    own_ref = tile_ref.reshape(comps, size, LANES)
    last_ref = side_ref.reshape(comps, face, LANES)
    nothing = jnp.zeros((face, LANES), bf16)
    columns = fill_columns(
        stack_ref, speed_ref, copy_ref,
        lambda v: own_ref[v],
        lambda v: last_ref[v],
        lambda v: nothing,
        lambda v: nothing,
        comps,
    )
    slots = trace_ref.shape[0]
    for v in columns:
        value = jnp.dot(first_ref[...], stack_ref[...], preferred_element_type=f32)
        at = slice(v * nodes, (v + 1) * nodes)
        trace_ref[:, at] = rhs_in[:, at] + time_step * value.T[:slots]
    for copy in copies[8:]:
        copy.wait()


def fill_columns(stack_ref, speed_ref, own_ref, own_at, last_at, edge_at, top_at, comps):
    size, width = speed_ref.shape[1:]
    face = size // Q
    for v in range(comps):
        own_ref[v] = own_at(v)
    for d in range(3):
        speed_ref[d] = advection[d] + own_ref[1 + d].astype(f32)
    lane = lax.broadcasted_iota(jnp.int32, (face, width), 1)
    for v in range(comps):
        own = own_ref[v]
        wide = own.astype(f32)
        for d in range(3):
            stack_ref[d * size : (d + 1) * size] = (wide * speed_ref[d]).astype(bf16)
        stack_ref[3 * size : 4 * size] = own
        last = pltpu.roll(last_at(v).astype(f32), 1, 1)
        edge = pltpu.roll(edge_at(v).astype(f32), 1, 1)
        edge = jnp.concatenate([edge] * (width // LANES), axis=1)
        stack_ref[4 * size : 4 * size + face] = jnp.where(lane == 0, edge, last).astype(bf16)
        stack_ref[4 * size + face :] = top_at(v)
        yield v


def outer_piece(tiles, sides, edge, top, full, after, result, start, stop, width):
    count, comps, size, _ = tiles.shape
    comps, faces, rows, _ = edge.shape
    face = faces * rows
    per_step = width // LANES
    held = (stop - start) * per_step
    shape = (comps, faces, Q, count, rows, LANES)

    def kernel(tiles_ref, sides_ref, edge_ref, top_ref, full_ref, *refs):
        out_ref, done_ref, stack_ref, speed_ref, copy_ref, held_ref, sem = refs[-7:]
        done_ref[...] = jnp.zeros_like(done_ref)
        behind_ref = edge_ref.reshape(comps, face, LANES)
        flat_ref = held_ref.reshape(held, comps, size, LANES)

        def joined(read):
            return jnp.concatenate([read(k) for k in range(per_step)], axis=1)

        def copy(i):
            return pltpu.make_async_copy(
                held_ref.at[i], out_ref.at[:, :, :, start * per_step + i], sem.at[i]
            )

        def step(n, carry):
            base = (start + n) * per_step
            columns = fill_columns(
                stack_ref, speed_ref, copy_ref,
                lambda v: joined(lambda k: tiles_ref[base + k, v]),
                lambda v: joined(lambda k: sides_ref[base + k, v]),
                lambda v: jnp.where(
                    base == 0, behind_ref[v].astype(f32), sides_ref[jnp.maximum(base - 1, 0), v].astype(f32)
                ),
                lambda v: joined(lambda k: top_ref[v, :, :, n * per_step + k].reshape(face, LANES)),
                comps,
            )
            for v in columns:
                value = jnp.dot(full_ref[...], stack_ref[...], preferred_element_type=f32).astype(bf16)
                for k in range(per_step):
                    flat_ref[n * per_step + k, v] = value[:, k * LANES : (k + 1) * LANES]
            for k in range(per_step):
                copy(n * per_step + k).start()
            return carry

        lax.fori_loop(0, stop - start, step, 0)
        for i in range(held):
            copy(i).wait()

    operands = [tiles, sides, edge, top, full, after]
    specs = [in_vmem] * len(operands)
    aliases = {}
    if result is not None:
        operands.append(held_in_hbm(result))
        specs.append(in_hbm)
        aliases = {len(specs) - 1: 0}
    return pl.pallas_call(
        kernel,
        in_specs=specs,
        out_specs=[in_hbm, in_vmem],
        out_shape=[pltpu.HBM(shape, bf16), jax.ShapeDtypeStruct((8, LANES), f32)],
        scratch_shapes=[
            pltpu.VMEM((full.shape[1], width), bf16),
            pltpu.VMEM((3, size, width), f32),
            pltpu.VMEM((comps, size, width), bf16),
            pltpu.VMEM((held, comps, faces, Q, rows, LANES), bf16),
            pltpu.SemaphoreType.DMA((held,)),
        ],
        input_output_aliases=aliases,
        compiler_params=params,
        name="outer",
    )(*operands)


def split(value):
    high = value.astype(bf16)
    return high, (value - high.astype(f32)).astype(bf16)


def whole(reduce, value):
    return reduce(reduce(value, axis=0, keepdims=True), axis=1, keepdims=True)


def rescale(value):
    top = whole(jnp.max, jnp.abs(value))
    by = jnp.where(top > 0.0, jnp.ceil(jnp.log2(jnp.maximum(top, 1e-37))), 0.0)
    return value * jnp.exp2(-by), by


def whole_count(count_ref):
    return jnp.max(count_ref[...])


def apply_blocks(count, value_ref, block_at, out_ref):
    slots, order = value_ref.shape
    rows = lax.broadcasted_iota(jnp.int32, (2 * GROUP, order), 0)

    def group(g):
        block = block_at(g)
        here = slice(g * GROUP, (g + 1) * GROUP)
        terms = jnp.concatenate(split(value_ref[here, :]), axis=0)
        kept = jnp.zeros((2 * GROUP, order), f32)
        for s in range(GROUP):
            product = jnp.dot(terms, block(s), preferred_element_type=f32)
            kept = jnp.where((rows == s) | (rows == s + GROUP), product, kept)
        out_ref[here, :] = kept[:GROUP] + kept[GROUP:]

    group(0)
    for g in range(1, slots // GROUP):
        pl.when(g * GROUP < count)(lambda g=g: group(g))

        @pl.when(g * GROUP >= count)
        def _(g=g):
            out_ref[g * GROUP : (g + 1) * GROUP, :] = jnp.zeros((GROUP, order), f32)


def emit(direction_ref, exponent, sent_ref, exponent_ref):
    slots, order = direction_ref.shape
    exponent_ref[...] = jnp.broadcast_to(exponent, exponent_ref.shape)
    sent_ref[:, :order] = direction_ref[...].astype(bf16)
    sent_ref[:, order:] = jnp.broadcast_to(exponent, (slots, sent_ref.shape[1] - order)).astype(bf16)


def live_rows(count, shape):
    return (lax.broadcasted_iota(jnp.int32, shape, 0) < count).astype(f32)


def turn_kernel(count_ref, near_ref, far_ref, state_ref, after_ref, turned_ref, tiles_ref, sides_ref, sem):
    tiles = tiles_ref.shape[0]
    copies = [pltpu.make_async_copy(state_ref.at[:, :, :, t], tiles_ref.at[t], sem.at[t]) for t in range(tiles)]
    copies += [
        pltpu.make_async_copy(state_ref.at[:, :, Q - 1, t], sides_ref.at[t], sem.at[tiles + t]) for t in range(tiles)
    ]
    for copy in copies:
        copy.start()

    def near(s, carry):
        turned_ref[2 * s] = near_ref[2 * s].T
        turned_ref[2 * s + 1] = near_ref[2 * s + 1].T
        return carry

    def far(s, carry):
        turned_ref[GROUP + 2 * s] = far_ref[2 * s].T
        turned_ref[GROUP + 2 * s + 1] = far_ref[2 * s + 1].T
        return carry

    lax.fori_loop(0, GROUP // 2, near, 0)

    @pl.when(whole_count(count_ref) > GROUP)
    def _():
        lax.fori_loop(0, far_ref.shape[0] // 2, far, 0)

    for copy in copies:
        copy.wait()


def start_kernel(
    count_ref, blocks_in_ref, near_ref, edge_ref, corner_ref, first_ref, rhs_ref,
    basis_ref, direction_ref, sent_ref, exponent_ref, far_ref,
    stack_ref, trace_ref, block_sem,
):
    slots, order = rhs_ref.shape
    comps, faces, rows, _ = edge_ref.shape
    count = whole_count(count_ref)

    def block_copy(g):
        source = blocks_in_ref.at[pl.ds(g * GROUP, GROUP)]
        return pltpu.make_async_copy(source, far_ref.at[pl.ds((g - 1) * GROUP, GROUP)], block_sem.at[g])

    def arrived(g):
        if g == 0:
            return lambda s: near_ref[s].T
        block_copy(g).wait()
        return lambda s: far_ref[(g - 1) * GROUP + s].T

    for g in range(1, slots // GROUP):
        pl.when(g * GROUP < count)(block_copy(g).start)
    nodes = order // comps
    face = faces * rows
    behind_ref = edge_ref.reshape(comps, face, LANES)
    below_ref = corner_ref.reshape(comps, face, LANES)
    lane = lax.broadcasted_iota(jnp.int32, (face, LANES), 1)
    weights = first_ref[:, first_ref.shape[1] - 2 * face :]
    for v in range(comps):
        edge = pltpu.roll(behind_ref[v].astype(f32), 1, 1)
        stack_ref[:face] = jnp.where(lane == 0, edge, 0.0).astype(bf16)
        stack_ref[face:] = below_ref[v]
        value = jnp.dot(weights, stack_ref[...], preferred_element_type=f32)
        trace_ref[:, v * nodes : (v + 1) * nodes] = value.T[:slots]
    rhs = live_rows(count, rhs_ref.shape) * (rhs_ref[...] + time_step * trace_ref[...])
    basis, exponent = rescale(rhs)
    basis_ref[...] = basis
    apply_blocks(count, basis_ref, arrived, direction_ref)
    emit(direction_ref, exponent, sent_ref, exponent_ref)


def operate(count_ref, direction_ref, exponent_ref, one_ref, two_ref, sigma_ref, stiff_ref):
    slots, order = direction_ref.shape
    direction = direction_ref[...]
    high, low = split(direction)
    both = jnp.dot(jnp.concatenate([high, low], axis=0), stiff_ref[0], preferred_element_type=f32)
    stiff = both[:slots] + both[slots:] + jnp.dot(high, stiff_ref[1], preferred_element_type=f32)
    exponent = exponent_ref[0:1, 0:1]
    exponent_one = jnp.max(one_ref[0:1, order:].astype(f32), axis=1, keepdims=True)
    exponent_two = jnp.max(two_ref[0:1, order:].astype(f32), axis=1, keepdims=True)
    common = jnp.maximum(exponent, jnp.maximum(exponent_one, exponent_two))
    own = direction + time_step * (sigma_ref[...] * direction + stiff)
    one = one_ref[:, :order].astype(f32) * jnp.exp2(exponent_one - common)
    two = two_ref[:, :order].astype(f32) * jnp.exp2(exponent_two - common)
    image = own * jnp.exp2(exponent - common) - coupling * (one + two)
    basis, by = rescale(live_rows(whole_count(count_ref), image.shape) * image)
    return basis, common + by


def middle_kernel(
    count_ref, previous_ref, previous_exponent_ref, one_ref, two_ref, sigma_ref, stiff_ref, blocks_ref, _,
    basis_ref, direction_ref, sent_ref, exponent_ref,
):
    basis, exponent = operate(
        count_ref, previous_ref, previous_exponent_ref, one_ref, two_ref, sigma_ref, stiff_ref
    )
    basis_ref[...] = basis
    apply_blocks(whole_count(count_ref), basis_ref, lambda g: lambda s: blocks_ref[g * GROUP + s], direction_ref)
    emit(direction_ref, exponent, sent_ref, exponent_ref)


def pairs():
    return [(k, l) for k in range(ITERS + 1) for l in range(k, ITERS + 1)]


def gram_kernel(count_ref, _, previous_ref, *refs):
    exponent_refs, refs = refs[:ITERS], refs[ITERS:]
    one_ref, two_ref, sigma_ref, stiff_ref = refs[:4]
    basis_refs, part_ref = refs[4:-1], refs[-1]
    last, exponent = operate(
        count_ref, previous_ref, exponent_refs[-1], one_ref, two_ref, sigma_ref, stiff_ref
    )
    basis = [ref[...] for ref in basis_refs] + [last]
    lane = lax.broadcasted_iota(jnp.int32, (1, LANES), 1)
    row = jnp.zeros((1, LANES), f32)
    values = [whole(jnp.sum, basis[k] * basis[l]) for k, l in pairs()]
    values += [ref[0:1, 0:1] for ref in exponent_refs] + [exponent]
    for at, value in enumerate(values):
        row = jnp.where(lane == at, value, row)
    part_ref[...] = jnp.broadcast_to(row[None], part_ref.shape)


def finish_kernel(parts_ref, *refs):
    exponent_refs, direction_refs, out_ref = refs[:ITERS], refs[ITERS:-1], refs[-1]
    parts = parts_ref[:, 0, :]
    index = {pair: at for at, pair in enumerate(pairs())}
    count = ITERS + 1
    exponents = [parts[:, len(index) + k : len(index) + k + 1] for k in range(count)]
    tops = [jnp.max(e, axis=0, keepdims=True) for e in exponents]
    factors = [jnp.exp2(e - top) for e, top in zip(exponents, tops)]
    gram = {
        (k, l): jnp.sum(parts[:, at : at + 1] * factors[k] * factors[l], axis=0, keepdims=True)
        for (k, l), at in index.items()
    }
    scale = [lax.rsqrt(jnp.maximum(gram[k, k], 1e-37)) for k in range(count)]
    matrix = {(k, l): gram[k, l] * scale[k] * scale[l] for k, l in index}
    lower, inverse, middle = {}, [], []
    for k in range(ITERS):
        pivot = matrix[k + 1, k + 1]
        right = matrix[0, k + 1]
        for p in range(k):
            pivot = pivot - lower[k, p] * lower[k, p]
            right = right - lower[k, p] * middle[p]
        inverse.append(jnp.where(pivot > 5e-7, lax.rsqrt(jnp.maximum(pivot, 5e-7)), 0.0))
        for l in range(k + 1, ITERS):
            value = matrix[k + 1, l + 1]
            for p in range(k):
                value = value - lower[l, p] * lower[k, p]
            lower[l, k] = value * inverse[k]
        middle.append(right * inverse[k])
    weights = [None] * ITERS
    for k in reversed(range(ITERS)):
        value = middle[k]
        for l in range(k + 1, ITERS):
            value = value - lower[l, k] * weights[l]
        weights[k] = value * inverse[k]
    norm = gram[0, 0] * scale[0]
    total = None
    for k in range(ITERS):
        shift = jnp.exp2(tops[0] - tops[k + 1] + exponent_refs[k][0:1, 0:1])
        term = (weights[k] * scale[k + 1] * norm * shift) * direction_refs[k][...]
        total = term if total is None else total + term
    out_ref[...] = total


def solve(outer_state, derivative, stiffness, wall_rhs, wall_sigma, wall_inverse, wall_count):
    comps, nodes, rows, cols = outer_state.shape
    slots, order = wall_rhs.shape
    faces = nodes // Q
    size = nodes * rows
    state = held_in_hbm(tile_view(outer_state.reshape(comps, faces, Q, rows, cols)))
    count = cols // LANES
    edge, corner = pl.pallas_call(
        faces_kernel,
        in_specs=[in_hbm],
        out_specs=[in_vmem] * 2,
        out_shape=[
            jax.ShapeDtypeStruct((comps, faces, rows, LANES), bf16),
            jax.ShapeDtypeStruct((comps, Q, Q, rows, LANES), bf16),
        ],
        scratch_shapes=[pltpu.SemaphoreType.DMA((Q + 1,))],
        compiler_params=params,
        name="faces",
    )(state)
    came_corner = lax.ppermute(corner, "gy", ring("gy", 1))
    came_edge = lax.ppermute(edge, "gx", ring("gx", 1))

    jumps = jump_matrix(nodes, rows)
    depth = 3 * size + jumps.shape[1]
    expand = np.repeat(np.eye(nodes, dtype=np.float32), rows, axis=0)
    jumps = np.concatenate([jumps, jumps[::rows]])
    operands = (
        state, wall_inverse, wall_rhs, wall_sigma, derivative, stiffness, jnp.asarray(expand, bf16),
        jnp.asarray(jumps, bf16),
    )
    half_shape = jax.ShapeDtypeStruct((comps, Q, Q, count // 2, rows, LANES), bf16)
    operands = tuple(held_in_hbm(operand) for operand in operands)
    rhs, sigma, full, first, stiff, low, high, blocks = pl.pallas_call(
        prep_kernel,
        in_specs=[in_hbm] * len(operands),
        out_specs=[in_vmem] * 8,
        out_shape=[
            jax.ShapeDtypeStruct(wall_rhs.shape, f32),
            jax.ShapeDtypeStruct(wall_sigma.shape, f32),
            jax.ShapeDtypeStruct((size, depth), bf16),
            jax.ShapeDtypeStruct((nodes, depth), bf16),
            jax.ShapeDtypeStruct((2, order, order), bf16),
            half_shape,
            half_shape,
            jax.ShapeDtypeStruct((GROUP, order, order), bf16),
        ],
        scratch_shapes=[pltpu.VMEM(a.shape, a.dtype) for a in (wall_rhs, derivative, stiffness)]
        + [pltpu.VMEM(expand.shape, bf16), pltpu.VMEM(jumps.shape, bf16)]
        + [pltpu.VMEM((comps, faces, Q, rows, LANES), bf16), pltpu.VMEM(edge.shape, bf16)]
        + [pltpu.VMEM((depth, LANES), bf16), pltpu.VMEM((3, size, LANES), f32), pltpu.VMEM((comps, size, LANES), bf16)]
        + [pltpu.SemaphoreType.DMA((9 + 2 * Q,))],
        compiler_params=params,
        name="prep",
    )(*operands)

    vector = jax.ShapeDtypeStruct((slots, order), f32)
    padded = -(-(order + 1) // LANES) * LANES
    step_shapes = [
        vector, vector, jax.ShapeDtypeStruct((slots, padded), bf16), jax.ShapeDtypeStruct((8, LANES), f32),
    ]
    basis, direction, sent, exponent, far = pl.pallas_call(
        start_kernel,
        in_specs=[in_vmem, in_hbm] + [in_vmem] * 5,
        out_specs=[in_vmem] * 5,
        out_shape=step_shapes + [jax.ShapeDtypeStruct((slots - GROUP, order, order), bf16)],
        scratch_shapes=[
            pltpu.VMEM((2 * faces * rows, LANES), bf16), pltpu.VMEM((slots, order), f32),
            pltpu.SemaphoreType.DMA((slots // GROUP,)),
        ],
        compiler_params=params,
        name="start",
    )(wall_count, held_in_hbm(wall_inverse), blocks, came_edge, came_corner, first, rhs)
    bases, directions, exponents = [basis], [direction], [exponent]

    width = 2 * LANES
    steps = cols // width
    bounds = [steps * k // (ITERS - 1) for k in range(ITERS)]
    residual, done = None, exponent
    for k in range(ITERS):
        one, two = neighbours(sent, "gx")
        if k == 0:
            came_top = [lax.ppermute(low, "gy", ring("gy", 1))]
            came_top.append(lax.ppermute(high, "gy", ring("gy", 1)))
            blocks, tiles, sides = pl.pallas_call(
                turn_kernel,
                in_specs=[in_vmem] * 3 + [in_hbm, in_vmem],
                out_specs=[in_vmem] * 3,
                out_shape=[
                    jax.ShapeDtypeStruct(wall_inverse.shape, bf16),
                    jax.ShapeDtypeStruct((count, comps, faces, Q, rows, LANES), bf16),
                    jax.ShapeDtypeStruct((count, *edge.shape), bf16),
                ],
                scratch_shapes=[pltpu.SemaphoreType.DMA((2 * count,))],
                compiler_params=params,
                name="turn",
            )(wall_count, blocks, far, state, exponent)
            tiles = tiles.reshape(count, comps, size, LANES)
            sides = sides.reshape(count, comps, faces * rows, LANES)
        else:
            residual, done = outer_piece(
                tiles, sides, came_edge, came_top[k - 1], full, exponent, residual, bounds[k - 1], bounds[k], width
            )
        if k < ITERS - 1:
            basis, direction, sent, exponent = pl.pallas_call(
                middle_kernel,
                in_specs=[in_vmem] + [in_vmem] * 8,
                out_specs=[in_vmem] * 4,
                out_shape=step_shapes,
                compiler_params=params,
                name="middle",
            )(wall_count, direction, exponent, one, two, sigma, stiff, blocks, done)
            bases.append(basis)
            directions.append(direction)
            exponents.append(exponent)

    devices = lax.axis_size("gx") * lax.axis_size("gy")
    part = pl.pallas_call(
        gram_kernel,
        in_specs=[in_vmem] + [in_vmem] * (6 + 2 * ITERS),
        out_specs=in_vmem,
        out_shape=jax.ShapeDtypeStruct((devices, 1, LANES), f32),
        compiler_params=params,
        name="gram",
    )(wall_count, done, direction, *exponents, one, two, sigma, stiff, *bases)
    parts = lax.all_to_all(part, ("gx", "gy"), 0, 0)
    wall_update = pl.pallas_call(
        finish_kernel,
        in_specs=[in_vmem] * (1 + 2 * ITERS),
        out_specs=in_vmem,
        out_shape=vector,
        compiler_params=params,
        name="finish",
    )(parts, *exponents, *directions)
    return from_tile_view(residual).reshape(outer_state.shape), wall_update


def solution(mesh):
    in_specs = (
        P(None, None, "gy", "gx"),
        P(),
        P(),
        P(("gx", "gy"), None),
        P(("gx", "gy"), None),
        P(("gx", "gy"), None, None),
        P("gx", "gy"),
    )
    out_specs = (P(None, None, "gy", "gx"), P(("gx", "gy"), None))
    return jax.shard_map(solve, mesh=mesh, in_specs=in_specs, out_specs=out_specs, check_vma=False)
```

```python
import jax
import jax.numpy as jnp
import numpy as np
from jax import lax
from jax.experimental import pallas as pl
from jax.experimental.pallas import tpu as pltpu
from jax.sharding import PartitionSpec as P


Q = 4
ITERS = 3

time_step = 0.3
coupling = 0.25
upwind_x = 2.0
upwind_y = 1.0
advection = (1.0, 0.5, 0.25)

LANES = 128
GROUP = 16
UNROLL = 8
VMEM_BYTES = 24 << 20
bf16 = jnp.bfloat16
f32 = jnp.float32

in_vmem = pl.BlockSpec(memory_space=pltpu.VMEM)
in_hbm = pl.BlockSpec(memory_space=pltpu.HBM)
params = pltpu.CompilerParams(vmem_limit_bytes=VMEM_BYTES)


def held_in_hbm(array):
    return pltpu.with_memory_space_constraint(array, pltpu.HBM)


def ring(axis, by):
    count = lax.axis_size(axis)
    return [(i, (i + by) % count) for i in range(count)]


def neighbours(array, axis):
    count = lax.axis_size(axis)
    if count % 2 or count < 4:
        first, second = ring(axis, 1), ring(axis, -1)
    else:
        first = [(i, i ^ 1) for i in range(count)]
        second = [(i, (i + (1 if i % 2 else -1)) % count) for i in range(count)]
    one = lax.ppermute(array, axis, first)
    two = lax.ppermute(array, axis, second)
    return one, two


def jump_matrix(nodes, rows):
    faces = nodes // Q
    out = np.zeros((nodes * rows, nodes * rows + 2 * faces * rows), np.float32)
    for m in range(nodes):
        i, j, k = m % Q, m // Q % Q, m // (Q * Q)
        for r in range(rows):
            row = m * rows + r
            if i == 0:
                out[row, row] -= upwind_x
                out[row, nodes * rows + (m // Q) * rows + r] += upwind_x
            if j == 0:
                out[row, row] -= upwind_y
                if r > 0:
                    out[row, (m + Q * (Q - 1)) * rows + r - 1] += upwind_y
                else:
                    column = (k * Q + i) * rows + rows - 1
                    out[row, (nodes + faces) * rows + column] += upwind_y
    return out


def tile_view(array):
    *lead, rows, cols = array.shape
    return jnp.swapaxes(array.reshape(*lead, rows, cols // LANES, LANES), -3, -2)


def from_tile_view(array):
    *lead, tiles, rows, lanes = array.shape
    return jnp.swapaxes(array, -3, -2).reshape(*lead, rows, tiles * lanes)


def faces_kernel(state_ref, edge_ref, corner_ref, sem):
    tiles = state_ref.shape[3]
    copies = [pltpu.make_async_copy(state_ref.at[:, :, Q - 1, tiles - 1], edge_ref, sem.at[0])]
    for k in range(Q):
        rows = state_ref.at[:, pl.ds(k * Q + Q - 1, 1)]
        copies.append(pltpu.make_async_copy(rows.at[:, :, :, 0], corner_ref.at[:, pl.ds(k, 1)], sem.at[1 + k]))
    for copy in copies:
        copy.start()
    for copy in copies:
        copy.wait()


def prep_kernel(
    state_ref, blocks_in_ref, rhs_ref, sigma_ref, deriv_ref, stiff_ref, expand_ref, jump_ref,
    trace_ref, sigma_out_ref, full_ref, first_ref, block_ref, low_ref, high_ref, blocks_ref,
    rhs_in, deriv_in, stiff_in, expand_in, jump_in, tile_ref, side_ref, stack_ref, speed_ref, copy_ref, sem,
):
    pairs_of_refs = [
        (deriv_ref, deriv_in), (expand_ref, expand_in), (jump_ref, jump_in), (stiff_ref, stiff_in),
        (state_ref.at[:, :, :, 0], tile_ref), (state_ref.at[:, :, Q - 1, 0], side_ref),
        (rhs_ref, rhs_in), (sigma_ref, sigma_out_ref),
    ]
    pairs_of_refs.append((blocks_in_ref.at[pl.ds(0, blocks_ref.shape[0])], blocks_ref))
    half = low_ref.shape[3]
    for k in range(Q):
        rows_at = state_ref.at[:, pl.ds(k * Q + Q - 1, 1)]
        pairs_of_refs.append((rows_at.at[:, :, :, pl.ds(0, half)], low_ref.at[:, pl.ds(k, 1)]))
        pairs_of_refs.append((rows_at.at[:, :, :, pl.ds(half, half)], high_ref.at[:, pl.ds(k, 1)]))
    copies = [pltpu.make_async_copy(a, b, sem.at[at]) for at, (a, b) in enumerate(pairs_of_refs)]
    for copy in copies:
        copy.start()
    for copy in copies[:4]:
        copy.wait()
    size, nodes = expand_in.shape
    rows = size // nodes
    expand = expand_in[...]
    same = lax.broadcasted_iota(jnp.int32, (size, size), 0) % rows
    same = same == lax.broadcasted_iota(jnp.int32, (size, size), 1) % rows
    own = lax.broadcasted_iota(jnp.int32, (nodes, size), 1) % rows == 0
    for d in range(3):
        wide = lax.dot_general(
            deriv_in[d], expand, (((1,), (1,)), ((), ())), preferred_element_type=f32
        ).astype(bf16)
        both = jnp.dot(expand, wide, preferred_element_type=f32)
        full_ref[:, d * size : (d + 1) * size] = jnp.where(same, both, 0.0).astype(bf16)
        first_ref[:, d * size : (d + 1) * size] = jnp.where(own, wide.astype(f32), 0.0).astype(bf16)
    jump = jump_in[...]
    below = lax.broadcasted_iota(jnp.int32, jump.shape, 1) >= jump.shape[1] - size // Q
    jump = jnp.where(below & (lax.axis_index("gy") == 0), 0.0, jump.astype(f32)).astype(bf16)
    full_ref[:, 3 * size :] = jump[:size]
    first_ref[:, 3 * size :] = jump[size:]
    block_ref[...] = jnp.zeros_like(block_ref)
    high, low = split(stiff_in[...])
    for v in range(block_ref.shape[1] // nodes):
        at = slice(v * nodes, (v + 1) * nodes)
        block_ref[0, at, at] = high
        block_ref[1, at, at] = low
    for copy in copies[4:8]:
        copy.wait()
    comps, faces, _, _, _ = tile_ref.shape
    face = faces * rows
    own_ref = tile_ref.reshape(comps, size, LANES)
    last_ref = side_ref.reshape(comps, face, LANES)
    nothing = jnp.zeros((face, LANES), bf16)
    columns = fill_columns(
        stack_ref, speed_ref, copy_ref,
        lambda v: own_ref[v],
        lambda v: last_ref[v],
        lambda v: nothing,
        lambda v: nothing,
        comps,
    )
    slots = trace_ref.shape[0]
    for v in columns:
        value = jnp.dot(first_ref[...], stack_ref[...], preferred_element_type=f32)
        at = slice(v * nodes, (v + 1) * nodes)
        trace_ref[:, at] = rhs_in[:, at] + time_step * value.T[:slots]
    for copy in copies[8:]:
        copy.wait()


def fill_columns(stack_ref, speed_ref, own_ref, own_at, last_at, edge_at, top_at, comps):
    size, width = speed_ref.shape[1:]
    face = size // Q
    for v in range(comps):
        own_ref[v] = own_at(v)
    for d in range(3):
        speed_ref[d] = advection[d] + own_ref[1 + d].astype(f32)
    lane = lax.broadcasted_iota(jnp.int32, (face, width), 1)
    for v in range(comps):
        own = own_ref[v]
        wide = own.astype(f32)
        for d in range(3):
            stack_ref[d * size : (d + 1) * size] = (wide * speed_ref[d]).astype(bf16)
        stack_ref[3 * size : 4 * size] = own
        last = pltpu.roll(last_at(v).astype(f32), 1, 1)
        edge = pltpu.roll(edge_at(v).astype(f32), 1, 1)
        edge = jnp.concatenate([edge] * (width // LANES), axis=1)
        stack_ref[4 * size : 4 * size + face] = jnp.where(lane == 0, edge, last).astype(bf16)
        stack_ref[4 * size + face :] = top_at(v)
        yield v


def outer_piece(tiles, sides, edge, top, full, after, result, start, stop, width):
    count, comps, size, _ = tiles.shape
    comps, faces, rows, _ = edge.shape
    face = faces * rows
    per_step = width // LANES
    held = (stop - start) * per_step
    shape = (comps, faces, Q, count, rows, LANES)

    def kernel(tiles_ref, sides_ref, edge_ref, top_ref, full_ref, *refs):
        out_ref, done_ref, stack_ref, speed_ref, copy_ref, held_ref, sem = refs[-7:]
        done_ref[...] = jnp.zeros_like(done_ref)
        behind_ref = edge_ref.reshape(comps, face, LANES)
        flat_ref = held_ref.reshape(held, comps, size, LANES)

        def joined(read):
            return jnp.concatenate([read(k) for k in range(per_step)], axis=1)

        def copy(i):
            return pltpu.make_async_copy(
                held_ref.at[i], out_ref.at[:, :, :, start * per_step + i], sem.at[i]
            )

        def step(n, carry):
            base = (start + n) * per_step
            columns = fill_columns(
                stack_ref, speed_ref, copy_ref,
                lambda v: joined(lambda k: tiles_ref[base + k, v]),
                lambda v: joined(lambda k: sides_ref[base + k, v]),
                lambda v: jnp.where(
                    base == 0, behind_ref[v].astype(f32), sides_ref[jnp.maximum(base - 1, 0), v].astype(f32)
                ),
                lambda v: joined(lambda k: top_ref[v, :, :, n * per_step + k].reshape(face, LANES)),
                comps,
            )
            for v in columns:
                value = jnp.dot(full_ref[...], stack_ref[...], preferred_element_type=f32).astype(bf16)
                for k in range(per_step):
                    flat_ref[n * per_step + k, v] = value[:, k * LANES : (k + 1) * LANES]
            for k in range(per_step):
                copy(n * per_step + k).start()
            return carry

        lax.fori_loop(0, stop - start, step, 0)
        for i in range(held):
            copy(i).wait()

    operands = [tiles, sides, edge, top, full, after]
    specs = [in_vmem] * len(operands)
    aliases = {}
    if result is not None:
        operands.append(held_in_hbm(result))
        specs.append(in_hbm)
        aliases = {len(specs) - 1: 0}
    return pl.pallas_call(
        kernel,
        in_specs=specs,
        out_specs=[in_hbm, in_vmem],
        out_shape=[pltpu.HBM(shape, bf16), jax.ShapeDtypeStruct((8, LANES), f32)],
        scratch_shapes=[
            pltpu.VMEM((full.shape[1], width), bf16),
            pltpu.VMEM((3, size, width), f32),
            pltpu.VMEM((comps, size, width), bf16),
            pltpu.VMEM((held, comps, faces, Q, rows, LANES), bf16),
            pltpu.SemaphoreType.DMA((held,)),
        ],
        input_output_aliases=aliases,
        compiler_params=params,
        name="outer",
    )(*operands)


def split(value):
    high = value.astype(bf16)
    return high, (value - high.astype(f32)).astype(bf16)


def whole(reduce, value):
    return reduce(reduce(value, axis=0, keepdims=True), axis=1, keepdims=True)


def rescale(value):
    top = whole(jnp.max, jnp.abs(value))
    by = jnp.where(top > 0.0, jnp.ceil(jnp.log2(jnp.maximum(top, 1e-37))), 0.0)
    return value * jnp.exp2(-by), by


def whole_count(count_ref):
    return jnp.max(count_ref[...])


def in_groups(count, slots, group, clear):
    group(0)
    for g in range(1, slots // GROUP):
        pl.when(g * GROUP < count)(lambda g=g: group(g))
        pl.when(g * GROUP >= count)(lambda g=g: clear(g))


def apply_blocks(count, value_ref, blocks_of, out_ref):
    slots, order = value_ref.shape
    rows = lax.broadcasted_iota(jnp.int32, (2 * GROUP, order), 0) % GROUP

    def group(g):
        block = blocks_of(g)
        here = slice(g * GROUP, (g + 1) * GROUP)
        terms = jnp.concatenate(split(value_ref[here, :]), axis=0)
        kept = jnp.zeros((2 * GROUP, order), f32)
        for s in range(GROUP):
            kept = jnp.where(rows == s, jnp.dot(terms, block(s), preferred_element_type=f32), kept)
        out_ref[here, :] = kept[:GROUP] + kept[GROUP:]

    def clear(g):
        out_ref[g * GROUP : (g + 1) * GROUP, :] = jnp.zeros((GROUP, order), f32)

    in_groups(count, slots, group, clear)


def emit(direction_ref, exponent, sent_ref, exponent_ref):
    slots, order = direction_ref.shape
    exponent_ref[...] = jnp.broadcast_to(exponent, exponent_ref.shape)
    sent_ref[:, :order] = direction_ref[...].astype(bf16)
    sent_ref[:, order:] = jnp.broadcast_to(exponent, (slots, sent_ref.shape[1] - order)).astype(bf16)


def live_rows(count, shape):
    return (lax.broadcasted_iota(jnp.int32, shape, 0) < count).astype(f32)


def turn_kernel(count_ref, near_ref, far_ref, state_ref, after_ref, turned_ref, tiles_ref, sides_ref, sem):
    tiles = tiles_ref.shape[0]
    copies = [pltpu.make_async_copy(state_ref.at[:, :, :, t], tiles_ref.at[t], sem.at[t]) for t in range(tiles)]
    copies += [
        pltpu.make_async_copy(state_ref.at[:, :, Q - 1, t], sides_ref.at[t], sem.at[tiles + t]) for t in range(tiles)
    ]
    for copy in copies:
        copy.start()

    def turn(source_ref, source, target, count):
        def group(g, carry):
            for s in range(UNROLL):
                at = g * UNROLL + s
                turned_ref[target + at] = source_ref[source + at].T
            return carry

        lax.fori_loop(0, count // UNROLL, group, 0)

    near, far = near_ref.shape[0], far_ref.shape[0]
    turn(near_ref, 0, 0, GROUP)

    @pl.when(whole_count(count_ref) > GROUP)
    def _():
        turn(near_ref, GROUP, GROUP, near - GROUP)
        turn(far_ref, 0, near, far)

    for copy in copies:
        copy.wait()


def start_kernel(
    count_ref, blocks_in_ref, near_ref, edge_ref, corner_ref, first_ref, rhs_ref,
    basis_ref, direction_ref, sent_ref, exponent_ref, far_ref,
    stack_ref, trace_ref, turned_ref, far_sem,
):
    slots, order = rhs_ref.shape
    comps, faces, rows, _ = edge_ref.shape
    count = whole_count(count_ref)

    near = near_ref.shape[0]
    far_copy = pltpu.make_async_copy(blocks_in_ref.at[pl.ds(near, slots - near)], far_ref, far_sem)
    pl.when(count > GROUP)(far_copy.start)

    def blocks_of(g):
        def block(s):
            at = g * GROUP + s
            if at == near:
                far_copy.wait()
            own = near_ref[at] if at < near else far_ref[at - near]
            if s % 3 == 0:
                return own.T
            turned_ref[s] = own.T
            return turned_ref[s]

        return block

    nodes = order // comps
    face = faces * rows
    behind_ref = edge_ref.reshape(comps, face, LANES)
    below_ref = corner_ref.reshape(comps, face, LANES)
    lane = lax.broadcasted_iota(jnp.int32, (face, LANES), 1)
    weights = first_ref[:, first_ref.shape[1] - 2 * face :]
    for v in range(comps):
        edge = pltpu.roll(behind_ref[v].astype(f32), 1, 1)
        stack_ref[:face] = jnp.where(lane == 0, edge, 0.0).astype(bf16)
        stack_ref[face:] = below_ref[v]
        value = jnp.dot(weights, stack_ref[...], preferred_element_type=f32)
        trace_ref[:, v * nodes : (v + 1) * nodes] = value.T[:slots]
    rhs = live_rows(count, rhs_ref.shape) * (rhs_ref[...] + time_step * trace_ref[...])
    basis, exponent = rescale(rhs)
    basis_ref[...] = basis
    apply_blocks(count, basis_ref, blocks_of, direction_ref)
    emit(direction_ref, exponent, sent_ref, exponent_ref)


def operate(count_ref, direction_ref, exponent_ref, one_ref, two_ref, sigma_ref, stiff_ref):
    slots, order = direction_ref.shape
    direction = direction_ref[...]
    high, low = split(direction)
    both = jnp.dot(jnp.concatenate([high, low], axis=0), stiff_ref[0], preferred_element_type=f32)
    stiff = both[:slots] + both[slots:] + jnp.dot(high, stiff_ref[1], preferred_element_type=f32)
    exponent = exponent_ref[0:1, 0:1]
    exponent_one = jnp.max(one_ref[0:1, order:].astype(f32), axis=1, keepdims=True)
    exponent_two = jnp.max(two_ref[0:1, order:].astype(f32), axis=1, keepdims=True)
    common = jnp.maximum(exponent, jnp.maximum(exponent_one, exponent_two))
    own = direction + time_step * (sigma_ref[...] * direction + stiff)
    one = one_ref[:, :order].astype(f32) * jnp.exp2(exponent_one - common)
    two = two_ref[:, :order].astype(f32) * jnp.exp2(exponent_two - common)
    image = own * jnp.exp2(exponent - common) - coupling * (one + two)
    basis, by = rescale(live_rows(whole_count(count_ref), image.shape) * image)
    return basis, common + by


def middle_kernel(
    count_ref, previous_ref, previous_exponent_ref, one_ref, two_ref, sigma_ref, stiff_ref, blocks_ref, _,
    basis_ref, direction_ref, sent_ref, exponent_ref,
):
    basis, exponent = operate(
        count_ref, previous_ref, previous_exponent_ref, one_ref, two_ref, sigma_ref, stiff_ref
    )
    basis_ref[...] = basis
    apply_blocks(
        whole_count(count_ref), basis_ref, lambda g: lambda s: blocks_ref[g * GROUP + s], direction_ref
    )
    emit(direction_ref, exponent, sent_ref, exponent_ref)


def pairs():
    return [(k, l) for k in range(ITERS + 1) for l in range(k, ITERS + 1)]


def gram_kernel(count_ref, _, previous_ref, *refs):
    exponent_refs, refs = refs[:ITERS], refs[ITERS:]
    one_ref, two_ref, sigma_ref, stiff_ref = refs[:4]
    basis_refs, part_ref = refs[4:-1], refs[-1]
    last, exponent = operate(
        count_ref, previous_ref, exponent_refs[-1], one_ref, two_ref, sigma_ref, stiff_ref
    )
    basis = [ref[...] for ref in basis_refs] + [last]
    lane = lax.broadcasted_iota(jnp.int32, (1, LANES), 1)
    row = jnp.zeros((1, LANES), f32)
    values = [whole(jnp.sum, basis[k] * basis[l]) for k, l in pairs()]
    values += [ref[0:1, 0:1] for ref in exponent_refs] + [exponent]
    for at, value in enumerate(values):
        row = jnp.where(lane == at, value, row)
    part_ref[...] = jnp.broadcast_to(row[None], part_ref.shape)


def finish_kernel(parts_ref, *refs):
    exponent_refs, direction_refs, out_ref = refs[:ITERS], refs[ITERS:-1], refs[-1]
    parts = parts_ref[:, 0, :]
    index = {pair: at for at, pair in enumerate(pairs())}
    count = ITERS + 1
    exponents = [parts[:, len(index) + k : len(index) + k + 1] for k in range(count)]
    tops = [jnp.max(e, axis=0, keepdims=True) for e in exponents]
    factors = [jnp.exp2(e - top) for e, top in zip(exponents, tops)]
    gram = {
        (k, l): jnp.sum(parts[:, at : at + 1] * factors[k] * factors[l], axis=0, keepdims=True)
        for (k, l), at in index.items()
    }
    scale = [lax.rsqrt(jnp.maximum(gram[k, k], 1e-37)) for k in range(count)]
    matrix = {(k, l): gram[k, l] * scale[k] * scale[l] for k, l in index}
    lower, inverse, middle = {}, [], []
    for k in range(ITERS):
        pivot = matrix[k + 1, k + 1]
        right = matrix[0, k + 1]
        for p in range(k):
            pivot = pivot - lower[k, p] * lower[k, p]
            right = right - lower[k, p] * middle[p]
        inverse.append(jnp.where(pivot > 5e-7, lax.rsqrt(jnp.maximum(pivot, 5e-7)), 0.0))
        for l in range(k + 1, ITERS):
            value = matrix[k + 1, l + 1]
            for p in range(k):
                value = value - lower[l, p] * lower[k, p]
            lower[l, k] = value * inverse[k]
        middle.append(right * inverse[k])
    weights = [None] * ITERS
    for k in reversed(range(ITERS)):
        value = middle[k]
        for l in range(k + 1, ITERS):
            value = value - lower[l, k] * weights[l]
        weights[k] = value * inverse[k]
    norm = gram[0, 0] * scale[0]
    total = None
    for k in range(ITERS):
        shift = jnp.exp2(tops[0] - tops[k + 1] + exponent_refs[k][0:1, 0:1])
        term = (weights[k] * scale[k + 1] * norm * shift) * direction_refs[k][...]
        total = term if total is None else total + term
    out_ref[...] = total


def solve(outer_state, derivative, stiffness, wall_rhs, wall_sigma, wall_inverse, wall_count):
    comps, nodes, rows, cols = outer_state.shape
    slots, order = wall_rhs.shape
    faces = nodes // Q
    size = nodes * rows
    state = held_in_hbm(tile_view(outer_state.reshape(comps, faces, Q, rows, cols)))
    count = cols // LANES
    edge, corner = pl.pallas_call(
        faces_kernel,
        in_specs=[in_hbm],
        out_specs=[in_vmem] * 2,
        out_shape=[
            jax.ShapeDtypeStruct((comps, faces, rows, LANES), bf16),
            jax.ShapeDtypeStruct((comps, Q, Q, rows, LANES), bf16),
        ],
        scratch_shapes=[pltpu.SemaphoreType.DMA((Q + 1,))],
        compiler_params=params,
        name="faces",
    )(state)
    came_corner = lax.ppermute(corner, "gy", ring("gy", 1))
    came_edge = lax.ppermute(edge, "gx", ring("gx", 1))

    jumps = jump_matrix(nodes, rows)
    depth = 3 * size + jumps.shape[1]
    expand = np.repeat(np.eye(nodes, dtype=np.float32), rows, axis=0)
    jumps = np.concatenate([jumps, jumps[::rows]])
    operands = (
        state, wall_inverse, wall_rhs, wall_sigma, derivative, stiffness, jnp.asarray(expand, bf16),
        jnp.asarray(jumps, bf16),
    )
    near_slots = slots * 3 // 4
    half_shape = jax.ShapeDtypeStruct((comps, Q, Q, count // 2, rows, LANES), bf16)
    operands = tuple(held_in_hbm(operand) for operand in operands)
    rhs, sigma, full, first, stiff, low, high, blocks = pl.pallas_call(
        prep_kernel,
        in_specs=[in_hbm] * len(operands),
        out_specs=[in_vmem] * 8,
        out_shape=[
            jax.ShapeDtypeStruct(wall_rhs.shape, f32),
            jax.ShapeDtypeStruct(wall_sigma.shape, f32),
            jax.ShapeDtypeStruct((size, depth), bf16),
            jax.ShapeDtypeStruct((nodes, depth), bf16),
            jax.ShapeDtypeStruct((2, order, order), bf16),
            half_shape,
            half_shape,
            jax.ShapeDtypeStruct((near_slots, order, order), bf16),
        ],
        scratch_shapes=[pltpu.VMEM(a.shape, a.dtype) for a in (wall_rhs, derivative, stiffness)]
        + [pltpu.VMEM(expand.shape, bf16), pltpu.VMEM(jumps.shape, bf16)]
        + [pltpu.VMEM((comps, faces, Q, rows, LANES), bf16), pltpu.VMEM(edge.shape, bf16)]
        + [pltpu.VMEM((depth, LANES), bf16), pltpu.VMEM((3, size, LANES), f32), pltpu.VMEM((comps, size, LANES), bf16)]
        + [pltpu.SemaphoreType.DMA((9 + 2 * Q,))],
        compiler_params=params,
        name="prep",
    )(*operands)

    vector = jax.ShapeDtypeStruct((slots, order), f32)
    padded = -(-(order + 1) // LANES) * LANES
    step_shapes = [
        vector, vector, jax.ShapeDtypeStruct((slots, padded), bf16), jax.ShapeDtypeStruct((8, LANES), f32),
    ]
    basis, direction, sent, exponent, far = pl.pallas_call(
        start_kernel,
        in_specs=[in_vmem, in_hbm] + [in_vmem] * 5,
        out_specs=[in_vmem] * 5,
        out_shape=step_shapes + [jax.ShapeDtypeStruct((slots - near_slots, order, order), bf16)],
        scratch_shapes=[
            pltpu.VMEM((2 * faces * rows, LANES), bf16), pltpu.VMEM((slots, order), f32),
            pltpu.VMEM((GROUP, order, order), bf16),
            pltpu.SemaphoreType.DMA(()),
        ],
        compiler_params=params,
        name="start",
    )(wall_count, held_in_hbm(wall_inverse), blocks, came_edge, came_corner, first, rhs)
    bases, directions, exponents = [basis], [direction], [exponent]

    width = 2 * LANES
    steps = cols // width
    bounds = [steps * k // (ITERS - 1) for k in range(ITERS)]
    residual, done = None, exponent
    for k in range(ITERS):
        one, two = neighbours(sent, "gx")
        if k == 0:
            came_top = [lax.ppermute(low, "gy", ring("gy", 1))]
            came_top.append(lax.ppermute(high, "gy", ring("gy", 1)))
            blocks, tiles, sides = pl.pallas_call(
                turn_kernel,
                in_specs=[in_vmem] * 3 + [in_hbm, in_vmem],
                out_specs=[in_vmem] * 3,
                out_shape=[
                    jax.ShapeDtypeStruct(wall_inverse.shape, bf16),
                    jax.ShapeDtypeStruct((count, comps, faces, Q, rows, LANES), bf16),
                    jax.ShapeDtypeStruct((count, *edge.shape), bf16),
                ],
                scratch_shapes=[pltpu.SemaphoreType.DMA((2 * count,))],
                compiler_params=params,
                name="turn",
            )(wall_count, blocks, far, state, exponent)
            tiles = tiles.reshape(count, comps, size, LANES)
            sides = sides.reshape(count, comps, faces * rows, LANES)
        else:
            residual, done = outer_piece(
                tiles, sides, came_edge, came_top[k - 1], full, exponent, residual, bounds[k - 1], bounds[k], width
            )
        if k < ITERS - 1:
            basis, direction, sent, exponent = pl.pallas_call(
                middle_kernel,
                in_specs=[in_vmem] * 9,
                out_specs=[in_vmem] * 4,
                out_shape=step_shapes,
                compiler_params=params,
                name="middle",
            )(wall_count, direction, exponent, one, two, sigma, stiff, blocks, done)
            bases.append(basis)
            directions.append(direction)
            exponents.append(exponent)

    devices = lax.axis_size("gx") * lax.axis_size("gy")
    part = pl.pallas_call(
        gram_kernel,
        in_specs=[in_vmem] + [in_vmem] * (6 + 2 * ITERS),
        out_specs=in_vmem,
        out_shape=jax.ShapeDtypeStruct((devices, 1, LANES), f32),
        compiler_params=params,
        name="gram",
    )(wall_count, done, direction, *exponents, one, two, sigma, stiff, *bases)
    parts = lax.all_to_all(part, ("gx", "gy"), 0, 0)
    wall_update = pl.pallas_call(
        finish_kernel,
        in_specs=[in_vmem] * (1 + 2 * ITERS),
        out_specs=in_vmem,
        out_shape=vector,
        compiler_params=params,
        name="finish",
    )(parts, *exponents, *directions)
    return from_tile_view(residual).reshape(outer_state.shape), wall_update


def solution(mesh):
    in_specs = (
        P(None, None, "gy", "gx"),
        P(),
        P(),
        P(("gx", "gy"), None),
        P(("gx", "gy"), None),
        P(("gx", "gy"), None, None),
        P("gx", "gy"),
    )
    out_specs = (P(None, None, "gy", "gx"), P(("gx", "gy"), None))
    return jax.shard_map(solve, mesh=mesh, in_specs=in_specs, out_specs=out_specs, check_vma=False)
```
